32 devices in a mesh: group: 4 (over y, x), delay: 8 (over z, core).
Axes of the slice: x: 2, y: 2, z: 4, core: 2. Of those that a mesh axis runs over, the one named last changes fastest.
Arguments:
- retarded: bfloat16 [8, 16, 3, 256, 256], P('delay', 'group'), may hold values from -0.0625 to 0.0625
- block_row: int32 [8, 16, 3], P('delay', 'group'), may hold values from 0 to 3, as said below
- block_count: int32 [8, 16], P('delay', 'group'), may hold values from 1 to 3, as said below
- send_pick: int32 [8, 4, 4], P('delay'), may hold values from 0 to 3
- history: bfloat16 [8, 4096, 128], P('delay', 'group'), may hold values from -6 to 6
- incident: bfloat16 [4, 4096, 128], P(None, 'group'), may hold values from -6 to 6
- self_block: bfloat16 [4096, 1024], P('group'), may hold values from -0.1875 to 0.1875
- sheet_diag: float32 [4096], P('group'), may hold values from 1 to 1.6
Outputs:
- currents: bfloat16 [4, 4096, 128], P(None, 'group')
The draws below stay inside these ranges and needn't reach their ends.
Inputs may be any that keep to these rules, and one draw needn't show every extreme that they name: `block_row`: the live list places of one section, reading group and source group name distinct row blocks. `block_count`: list places at or beyond the count are ignored.
All inputs are finite; a program needn't handle non-finite values.
Results may differ from the reference program's by a relative error of at most 0.0085.
Values may be sent and summed in bfloat16 or wider, within the bound.
No kernel may reach another device: no remote copies, remote signals or barrier semaphores. Data moves between devices by JAX's collectives and lax.ppermute only.
A program may use at most 128 MiB of HBM per device.

```python
import math
import jax
import jax.numpy as jnp
from jax import lax

BLK = 256
GBLK = 4
LPG = 3
EXC = 128
STEPS = 4
ITERS = 3
GROUPS = 4
DELAYS = 8
GROUP_ROWS = 1024
UNKNOWNS = 4096


def draw_block_row(key, part):
    key_list = jax.random.split(jax.random.fold_in(key, 11), DELAYS * GROUPS * GROUPS)
    row_list = jax.vmap(lambda subkey: jax.random.permutation(subkey, GBLK)[:LPG])(key_list)
    return row_list.reshape(DELAYS, GROUPS * GROUPS, LPG).astype(jnp.int32)


def draw_block_count(key, part):
    key_cap, key_load = jax.random.split(jax.random.fold_in(key, 23))
    ceiling = jax.random.randint(key_cap, (DELAYS, GROUPS, 1), 1, LPG + 1)
    counts = jnp.minimum(jax.random.randint(key_load, (DELAYS, GROUPS, GROUPS), 1, LPG + 1), ceiling)
    section = lax.broadcasted_iota(jnp.int32, (DELAYS, GROUPS, GROUPS), 0)
    reader = lax.broadcasted_iota(jnp.int32, (DELAYS, GROUPS, GROUPS), 1)
    source = lax.broadcasted_iota(jnp.int32, (DELAYS, GROUPS, GROUPS), 2)
    forced = source == (reader + section) % GROUPS
    counts = jnp.where(forced, LPG, counts)
    return counts.reshape(DELAYS, GROUPS * GROUPS).astype(jnp.int32)


def draw_send_pick(key, part):
    return jax.random.randint(jax.random.fold_in(key, 37), (DELAYS, GROUPS, GROUPS), 0, GBLK).astype(jnp.int32)


def level_of(stream_key, dims, shards, low, top_value):
    def one(dim, parts):
        heights = jax.random.uniform(jax.random.fold_in(jax.random.fold_in(stream_key, 6), dim), (parts,), jnp.float32, low / len(shards), top_value / len(shards))
        return jnp.repeat(jnp.exp(heights), dims[dim] // parts).reshape((-1,) + (1,) * (len(dims) - dim - 1))

    level = one(*shards[0])
    for cut in shards[1:]:
        level = level * one(*cut)
    return level


def bell_draw(key, extent, scale, most, shards=(), held_as=jnp.bfloat16):
    array = jax.random.normal(key, extent, jnp.float32) * scale
    if len(shards) > 0:
        array = level_of(key, extent, shards, -0.22, 0.18) * array
    return jnp.clip(array, min=-most, max=most).astype(held_as)


def setup_inputs(seed: int = 0) -> dict:
    arg_keys = jax.random.split(jax.random.key(seed), 9)
    return {
        "retarded": bell_draw(arg_keys[0], (DELAYS, GROUPS * GROUPS, LPG, BLK, BLK), (DELAYS * GROUPS * BLK) ** -0.5, 0.0625, ((0, 8), (1, 4))),
        "block_row": draw_block_row(jax.random.fold_in(arg_keys[8], 71), 0),
        "block_count": draw_block_count(jax.random.fold_in(arg_keys[8], 71), 0),
        "send_pick": draw_send_pick(jax.random.fold_in(arg_keys[8], 71), 0),
        "history": bell_draw(arg_keys[4], (DELAYS, UNKNOWNS, EXC), 1.0, 6.0, ((0, 8), (1, 4))),
        "incident": bell_draw(arg_keys[5], (STEPS, UNKNOWNS, EXC), 1.0, 6.0, ((1, 4),)),
        "self_block": bell_draw(arg_keys[6], (UNKNOWNS, GROUP_ROWS), GROUP_ROWS ** -0.5, 0.1875, ((0, 4),)),
        "sheet_diag": jnp.clip(jnp.exp(math.log(1.6) - 0.47000364 * jax.random.uniform(arg_keys[7], (UNKNOWNS,), jnp.float32) ** level_of(arg_keys[7], (UNKNOWNS,), ((0, 4),), -0.2, 0.2)), 1.0, 1.6),
    }


def section_term(weights, row_list, live_count, picked, current):
    block_table = current.reshape(GROUPS * GBLK, BLK, EXC)
    block_index = (jnp.arange(GROUPS, dtype=jnp.int32) * GBLK + picked).astype(jnp.int32)
    blocks = block_table[block_index].astype(jnp.float32)
    terms = jnp.einsum("hlij,hjc->hlic", weights.astype(jnp.float32), blocks, precision=lax.Precision.HIGHEST)
    places = jnp.arange(LPG, dtype=jnp.int32)
    select = ((row_list[:, :, None] == jnp.arange(GBLK, dtype=jnp.int32)[None, None, :])
              & (places[None, :, None] < live_count[:, None, None])).astype(jnp.float32)
    summed = jnp.einsum("hlr,hlic->ric", select, terms, precision=lax.Precision.HIGHEST)
    return summed.reshape(GBLK * BLK, EXC)


def reference(retarded, block_row, block_count, send_pick, history, incident, self_block, sheet_diag):
    past_list = history
    results = []
    self_groups = self_block.astype(jnp.float32).reshape(GROUPS, GROUP_ROWS, GROUP_ROWS)
    for time_step in range(STEPS):
        def per_section(running, section):
            weights, row_list, live_count, picked, current = section
            weights = weights.reshape(GROUPS, GROUPS, LPG, BLK, BLK)
            row_list = row_list.reshape(GROUPS, GROUPS, LPG)
            live_count = live_count.reshape(GROUPS, GROUPS)
            reader_picks = jnp.transpose(picked)

            def per_group(inputs):
                return section_term(inputs[0], inputs[1], inputs[2], inputs[3], current)

            partial_value = lax.map(per_group, (weights, row_list, live_count, reader_picks))
            return running + partial_value.reshape(UNKNOWNS, EXC), None

        total_field, unused = lax.scan(per_section, jnp.zeros((UNKNOWNS, EXC), jnp.float32),
                                       (retarded, block_row, block_count, send_pick, past_list))
        driving = incident[time_step].astype(jnp.float32) - total_field
        diagonal = sheet_diag[:, None]
        iterate = driving / diagonal
        for sweep in range(ITERS):
            iterate_groups = iterate.astype(jnp.bfloat16).astype(jnp.float32).reshape(GROUPS, GROUP_ROWS, EXC)
            coupled = jnp.einsum("gij,gjc->gic", self_groups, iterate_groups, precision=lax.Precision.HIGHEST)
            iterate = (driving - coupled.reshape(UNKNOWNS, EXC)) / diagonal
        current = iterate.astype(jnp.bfloat16)
        results.append(current)
        past_list = jnp.concatenate([current[None], past_list[:-1]], axis=0)
    return jnp.stack(results)
```

```python
import functools

import jax
import jax.numpy as jnp
from jax import lax
from jax.experimental import pallas as pl
from jax.experimental.pallas import tpu as pltpu
from jax.sharding import PartitionSpec as P

STEPS = 4

F32 = jnp.float32
BF16 = jnp.bfloat16
VMEM = pl.BlockSpec(memory_space=pltpu.VMEM)
SMEM = pl.BlockSpec(memory_space=pltpu.SMEM)


def peer_of(group, hop, groups):
    return group ^ hop if groups & (groups - 1) == 0 else (group + hop) % groups


def source_of(group, hop, groups):
    return group ^ hop if groups & (groups - 1) == 0 else (group - hop) % groups


def call(kernel, out_shape, scalars, arrays, scratch=()):
    return pl.pallas_call(
        kernel,
        out_shape=out_shape,
        in_specs=[SMEM] * len(scalars) + [VMEM] * len(arrays),
        out_specs=jax.tree.map(lambda _: VMEM, out_shape),
        scratch_shapes=list(scratch),
    )(*scalars, *arrays)


def dot(a, b):
    return jnp.dot(a, b, preferred_element_type=F32)


def pick_kernel(groups, block, parts, place, picks, *refs):
    sources, outs = refs[:parts], refs[parts:]
    me = place[0]
    for hop in range(groups):
        start = pl.multiple_of(picks[me, peer_of(me, hop, groups)] * block, block)
        for part in range(parts):
            outs[hop][part * block : (part + 1) * block, :] = sources[part][pl.ds(start, block), :]


def dense_kernel(groups, block, depth, place, rows, counts, weights, dense):
    me = place[0]
    dense[...] = jnp.zeros_like(dense)
    for hop in range(groups):
        source = source_of(me, hop, groups)
        for entry in range(depth):

            @pl.when(entry < counts[0, source])
            def _():
                start = pl.multiple_of(rows[source, entry] * block, block)
                dense[pl.ds(start, block), hop * block : (hop + 1) * block] = weights[source, entry]


def sheet_kernel(self_block, column, row, dense, sheet, moved):
    scaled = self_block[...].astype(F32) * column[...]
    first = scaled.astype(BF16)
    second = dot(first, first)
    total = second - scaled
    third = dot(second.astype(BF16), first)
    sheet[...] = ((total - third) * row[...]).astype(BF16)
    width = sheet.shape[1]
    for start in range(0, dense.shape[1], width):
        size = min(width, dense.shape[1] - start)
        part = dense[:, start : start + size]
        moved[:, start : start + size] = (dot(sheet[...], part) + part.astype(F32) * column[...]).astype(BF16)


def product(matrix, blocks, part, block):
    total = None
    for hop, ref in enumerate(blocks):
        term = dot(matrix[:, hop * block : (hop + 1) * block], ref[part * block : (part + 1) * block, :])
        total = term if total is None else total + term
    return total


def term_kernel(groups, block, parts, matrix, *refs):
    blocks, out = refs[:groups], refs[groups]
    rows = matrix.shape[0]
    for part in range(parts):
        out[part * rows : (part + 1) * rows, :] = product(matrix, blocks, part, block).astype(out.dtype)


def driven_kernel(steps, sheet, column, incident, out):
    for step in range(1, steps):
        field = incident[step]
        out[step - 1] = field.astype(F32) * column[...] + dot(sheet[...], field)


def emit(groups, block, place, picks, current, passed, now, sends):
    @pl.when(place[1] == 0)
    def _():
        now[...] = current

    if passed is not None:

        @pl.when(place[1] != 0)
        def _():
            now[...] = passed

    else:

        @pl.when(place[1] != 0)
        def _():
            now[...] = jnp.zeros_like(now)

    me = place[0]
    for hop in range(len(sends)):
        start = pl.multiple_of(picks[me, peer_of(me, hop, groups)] * block, block)
        sends[hop][...] = now[pl.ds(start, block), :]


def first_kernel(groups, block, fields, place, picks, sheet, column, incident, *refs):
    terms, now, sends = refs[:fields], refs[fields], refs[fields + 1 :]
    total = terms[0][...].astype(F32)
    for ref in terms[1:]:
        total = total + ref[...].astype(F32)
    driving = incident[0].astype(F32) - total
    current = driving * column[...] + dot(sheet[...], driving.astype(BF16))
    emit(groups, block, place, picks, current.astype(BF16), None, now, sends)


def next_kernel(groups, block, fields, shifts, matrix_here, place, picks, driven, own, *refs):
    refs = list(refs)
    take = lambda count: [refs.pop(0) for _ in range(count)]
    blocks = take(groups) if matrix_here else []
    terms, passed = take(fields), take(shifts)
    now, sends = refs[0], refs[1:]
    value = driven[...] - (product(own, blocks, 0, block) if matrix_here else own[...])
    for ref in terms:
        value = value - ref[...].astype(F32)
    shifted = None
    for ref in passed:
        shifted = ref[...] if shifted is None else shifted + ref[...]
    emit(groups, block, place, picks, value.astype(BF16), shifted, now, sends)


def both_kernel(groups, block, matrix, *refs):
    blocks, wide, narrow = refs[:groups], refs[groups], refs[groups + 1]
    total = product(matrix, blocks, 0, block)
    wide[...] = total
    narrow[...] = total.astype(BF16)


def local(retarded, block_row, block_count, send_pick, history, incident, self_block, sheet_diag):
    groups = lax.axis_size("group")
    delays = lax.axis_size("delay")
    chips = delays // 2
    group_index = lax.axis_index("group")
    delay_index = lax.axis_index("delay")
    place = jnp.stack([group_index, delay_index]).astype(jnp.int32)
    weights = retarded[0]
    depth, block = weights.shape[1], weights.shape[-1]
    rows, columns = history.shape[1:]
    picks = send_pick[0]
    inverse = 1.0 / sheet_diag
    column, row = inverse[:, None], inverse[None, :]
    shape = jax.ShapeDtypeStruct
    piece = lambda parts=1: shape((parts * block, columns), BF16)

    def along(array, pairs):
        return lax.ppermute(array, "delay", pairs)

    def exchange(sends):
        return [sends[0]] + [
            lax.ppermute(sends[hop], "group", [(g, peer_of(g, hop, groups)) for g in range(groups)])
            for hop in range(1, groups)
        ]

    def picked(arrays):
        parts = len(arrays)
        return call(
            functools.partial(pick_kernel, groups, block, parts),
            [piece(parts)] * groups, (place, picks), arrays,
        )

    def plus(a, b):
        return (a.astype(F32) + b.astype(F32)).astype(BF16)

    def chip_sum(term):
        return plus(term, along(term, [(2 * z + 1, 2 * z) for z in range(chips)]))

    def chip_tree(term):
        stride = 1
        while stride < chips:
            pairs = [(2 * z, 2 * (z - stride)) for z in range(stride, chips, 2 * stride)]
            term = plus(term, along(term, pairs))
            stride *= 2
        return term

    def spread(current):
        return [along(current, [(0, 2 * z)]) for z in range(1, chips)]

    blocks = exchange(picked([history[0]]))
    shifted = []
    moving = history[0]
    for _ in range(1, STEPS):
        moving = along(moving, [(d, d + 1) for d in range(delays - 1)])
        shifted.append(moving)
    dense = call(
        functools.partial(dense_kernel, groups, block, depth),
        shape((rows, groups * block), BF16),
        (place, block_row[0], block_count), (weights,),
    )
    term = call(
        functools.partial(term_kernel, groups, block, 1), shape((rows, columns), BF16), (), (dense, *blocks)
    )
    chip = chip_sum(term)
    fields = [chip] + [along(chip, [(2 * z, 0)]) for z in range(1, chips)]

    sheet, matrix = call(
        sheet_kernel,
        (shape((rows, rows), BF16), shape((rows, groups * block), BF16)),
        (), (self_block, column, row, dense),
    )
    driven = call(
        functools.partial(driven_kernel, STEPS), shape((STEPS - 1, rows, columns), F32), (), (sheet, column, incident)
    )

    later = []
    for parts in ((shifted[0],), tuple(shifted[1:])):
        blocks = exchange(picked(list(parts)))
        term = call(
            functools.partial(term_kernel, groups, block, len(parts)),
            shape((len(parts) * rows, columns), BF16), (), (matrix, *blocks),
        )
        total = chip_tree(chip_sum(term))
        later += [total[k * rows : (k + 1) * rows] for k in range(len(parts))]

    whole = shape((rows, columns), BF16)
    outs = [whole] + [piece()] * groups
    current, *sends = call(
        functools.partial(first_kernel, groups, block, len(fields)),
        outs, (place, picks), (sheet, column, incident, *fields),
    )
    found = [current]
    near = along(current, [(0, 1)])
    spreads = [spread(current)]
    blocks = exchange(sends)
    current, *sends = call(
        functools.partial(next_kernel, groups, block, 1, 2, True),
        outs, (place, picks), (driven[0], matrix, *blocks, later[0], near, spreads[0][0]),
    )
    found.append(current)
    near = along(current, [(0, 1)])
    spreads.append(spread(current))

    blocks = exchange(sends)
    wide, narrow = call(
        functools.partial(both_kernel, groups, block), (shape((rows, columns), F32), whole), (), (matrix, *blocks)
    )
    from_next = along(narrow, [(1, 0)])
    from_second = along(narrow, [(2, 0)])
    current, *sends = call(
        functools.partial(next_kernel, groups, block, 2, 1, False),
        outs, (place, picks), (driven[1], wide, later[1], from_next, near),
    )
    found.append(current)
    spreads.append(spread(current))

    blocks = exchange(sends)
    wide, narrow = call(
        functools.partial(both_kernel, groups, block), (shape((rows, columns), F32), whole), (), (matrix, *blocks)
    )
    from_next = along(narrow, [(1, 0)])
    (current,) = call(
        functools.partial(next_kernel, groups, block, 3, 0, False),
        [whole], (place, picks), (driven[2], wide, later[2], from_next, from_second),
    )
    found.append(current)
    spreads.append(spread(current))

    results = []
    for current, copies in zip(found, spreads):
        far = functools.reduce(lambda a, b: a + b, copies)
        held = jnp.where(delay_index == 0, current, far)
        partner = along(held, [(2 * z, 2 * z + 1) for z in range(chips)])
        results.append(jnp.where(delay_index % 2 == 0, held, partner))
    return jnp.stack(results)


def solution(mesh):
    placed = (
        P("delay", "group", None, None, None),
        P("delay", "group", None),
        P("delay", "group"),
        P("delay", None, None),
        P("delay", "group", None),
        P(None, "group", None),
        P("group", None),
        P("group"),
    )
    return jax.shard_map(
        local, mesh=mesh, in_specs=placed, out_specs=P(None, "group", None), check_vma=False
    )
```

```python
import functools

import jax
import jax.numpy as jnp
from jax import lax
from jax.experimental import pallas as pl
from jax.experimental.pallas import tpu as pltpu
from jax.sharding import PartitionSpec as P

STEPS = 4

F32 = jnp.float32
BF16 = jnp.bfloat16
VMEM = pl.BlockSpec(memory_space=pltpu.VMEM)
SMEM = pl.BlockSpec(memory_space=pltpu.SMEM)


def peer_of(group, hop, groups):
    return group ^ hop if groups & (groups - 1) == 0 else (group + hop) % groups


def source_of(group, hop, groups):
    return group ^ hop if groups & (groups - 1) == 0 else (group - hop) % groups


def call(kernel, out_shape, scalars, arrays, spare=2):
    held = sum(a.size * a.dtype.itemsize for a in (*arrays, *jax.tree.leaves(out_shape)))
    return pl.pallas_call(
        kernel,
        out_shape=out_shape,
        in_specs=[SMEM] * len(scalars) + [VMEM] * len(arrays),
        out_specs=jax.tree.map(lambda _: VMEM, out_shape),
        compiler_params=pltpu.CompilerParams(vmem_limit_bytes=held + spare * (1 << 20)),
    )(*scalars, *arrays)


def dot(a, b):
    return jnp.dot(a, b, preferred_element_type=F32)


def pick_kernel(groups, block, parts, picks, *refs):
    sources, outs = refs[:parts], refs[parts:]
    for hop in range(groups):
        start = pl.multiple_of(picks[hop] * block, block)
        for part in range(parts):
            outs[hop][part * block : (part + 1) * block, :] = sources[part][pl.ds(start, block), :]


def dense_kernel(groups, block, depth, place, rows, counts, weights, dense):
    me = place[0]
    dense[...] = jnp.zeros_like(dense)
    for hop in range(groups):
        source = source_of(me, hop, groups)
        for entry in range(depth):

            @pl.when(entry < counts[0, source])
            def _():
                start = pl.multiple_of(rows[source, entry] * block, block)
                dense[pl.ds(start, block), hop * block : (hop + 1) * block] = weights[source, entry]


def sheet_kernel(self_block, column, row, dense, sheet, moved):
    scaled = self_block[...].astype(F32) * column[...]
    first = scaled.astype(BF16)
    second = dot(first, first)
    total = second - scaled
    third = dot(second.astype(BF16), first)
    sheet[...] = ((total - third) * row[...]).astype(BF16)
    width = sheet.shape[1]
    for start in range(0, dense.shape[1], width):
        size = min(width, dense.shape[1] - start)
        part = dense[:, start : start + size]
        moved[:, start : start + size] = (dot(sheet[...], part) + part.astype(F32) * column[...]).astype(BF16)


def product(matrix, blocks, part, block):
    total = None
    for hop, ref in enumerate(blocks):
        term = dot(matrix[:, hop * block : (hop + 1) * block], ref[part * block : (part + 1) * block, :])
        total = term if total is None else total + term
    return total


def term_kernel(groups, block, parts, matrix, *refs):
    blocks, out = refs[:groups], refs[groups]
    rows = matrix.shape[0]
    for part in range(parts):
        out[part * rows : (part + 1) * rows, :] = product(matrix, blocks, part, block).astype(out.dtype)


def driven_kernel(steps, sheet, column, incident, out):
    for step in range(1, steps):
        field = incident[step]
        out[step - 1] = field.astype(F32) * column[...] + dot(sheet[...], field)


def emit(block, sends, parts, picks, current):
    hops = len(sends)
    for part in range(parts):
        for hop in range(hops):
            start = pl.multiple_of(picks[part, hop] * block, block)
            sends[hop][part * block : (part + 1) * block, :] = current[pl.ds(start, block), :]


def first_kernel(groups, block, fields, picks, sheet, column, incident, *refs):
    terms, now, sends = refs[:fields], refs[fields], refs[fields + 1 :]
    total = terms[0][...].astype(F32)
    for ref in terms[1:]:
        total = total + ref[...].astype(F32)
    driving = incident[0].astype(F32) - total
    current = driving * column[...] + dot(sheet[...], driving.astype(BF16))
    now[...] = current.astype(BF16)
    emit(block, sends, 2, picks, now)


def next_kernel(groups, block, step, place, picks, driven, matrix, aside, *refs):
    refs = list(refs)
    take = lambda count: [refs.pop(0) for _ in range(count)]
    blocks = take(groups)
    older = take(groups) if step > 1 else None
    terms = take(1 if step < 3 else 2)
    passed = take(1) if step == 1 else None
    now = take(1)[0]
    if step == 2:
        own = take(1)[0]
    sends = refs
    near = product(matrix, blocks, 0, block)
    value = driven[step - 1] - near
    if step == 2:
        own[...] = near.astype(BF16)
    if step > 1:
        value = value - product(aside, older, 1, block)
    for ref in terms:
        value = value - ref[...].astype(F32)
    now[...] = value.astype(BF16)
    if sends:
        emit(block, sends, 2 if step == 1 else 1, picks, now)
    if passed is not None:

        @pl.when(place[1] == 2)
        def _():
            emit(block, sends, 1, picks, passed[0])


def local(retarded, block_row, block_count, send_pick, history, incident, self_block, sheet_diag):
    groups = lax.axis_size("group")
    delays = lax.axis_size("delay")
    chips = delays // 2
    group_index = lax.axis_index("group")
    delay_index = lax.axis_index("delay")
    place = jnp.stack([group_index, delay_index]).astype(jnp.int32)
    weights = retarded[0]
    depth, block = weights.shape[1], weights.shape[-1]
    rows, columns = history.shape[1:]
    inverse = 1.0 / sheet_diag
    column, row = inverse[:, None], inverse[None, :]
    shape = jax.ShapeDtypeStruct
    piece = lambda parts=1: shape((parts * block, columns), BF16)

    def along(array, pairs):
        return lax.ppermute(array, "delay", pairs)

    def swap(array):
        return along(array, [(d, d ^ 1) for d in range(delays)])

    def exchange(sends):
        return [sends[0]] + [
            lax.ppermute(sends[hop], "group", [(g, peer_of(g, hop, groups)) for g in range(groups)])
            for hop in range(1, groups)
        ]

    hops = jnp.stack([peer_of(group_index, hop, groups) for hop in range(groups)])
    mine = lax.dynamic_index_in_dim(send_pick[0], group_index, 0, keepdims=False)[hops]
    picks = jnp.stack([mine, swap(mine)])

    def picked(arrays):
        parts = len(arrays)
        return call(
            functools.partial(pick_kernel, groups, block, parts),
            [piece(parts)] * groups, (mine,), arrays,
        )

    def plus(a, b):
        return (a.astype(F32) + b.astype(F32)).astype(BF16)

    def chip_sum(term):
        return plus(term, swap(term))

    def chip_tree(term):
        stride = 1
        while stride < chips:
            pairs = [(2 * z, 2 * (z - stride)) for z in range(stride, chips, 2 * stride)]
            term = plus(term, along(term, pairs))
            stride *= 2
        return term

    def spread_tree(array):
        stride = 1
        while stride < chips:
            stride *= 2
        held = array
        z = delay_index // 2
        while stride > 1:
            stride //= 2
            pairs = [(2 * c, 2 * (c + stride)) for c in range(0, chips, 2 * stride) if c + stride < chips]
            got = along(held, pairs)
            held = jnp.where(z % (2 * stride) == stride, got, held)
        return held

    sends = picked([history[0]])
    blocks = exchange(sends)
    shifted = []
    moving, _ = lax.optimization_barrier((history[0], sends[0]))
    for _ in range(1, STEPS):
        moving = along(moving, [(d, d + 1) for d in range(delays - 1)])
        shifted.append(moving)
    dense = call(
        functools.partial(dense_kernel, groups, block, depth),
        shape((rows, groups * block), BF16),
        (place, block_row[0], block_count), (weights,),
    )
    term = call(
        functools.partial(term_kernel, groups, block, 1), shape((rows, columns), BF16), (), (dense, *blocks)
    )
    chip = chip_sum(term)
    fields = [chip] + [along(chip, [(2 * z, 0)]) for z in range(1, chips)]

    sheet, matrix = call(
        sheet_kernel,
        (shape((rows, rows), BF16), shape((rows, groups * block), BF16)),
        (), (self_block, column, row, dense), 8,
    )
    aside = swap(matrix)
    driven = call(
        functools.partial(driven_kernel, STEPS), shape((STEPS - 1, rows, columns), F32), (), (sheet, column, incident)
    )

    later = []
    for parts in ((shifted[0],), tuple(shifted[1:])):
        blocks = exchange(picked(list(parts)))
        term = call(
            functools.partial(term_kernel, groups, block, len(parts)),
            shape((len(parts) * rows, columns), BF16), (), (matrix, *blocks),
        )
        total = chip_tree(chip_sum(term))
        later += [total[k * rows : (k + 1) * rows] for k in range(len(parts))]

    whole = shape((rows, columns), BF16)
    current, *sends = call(
        functools.partial(first_kernel, groups, block, len(fields)),
        [whole] + [piece(2)] * groups, (picks,), (sheet, column, incident, *fields),
    )
    found = [current]
    second = along(current, [(0, 2)])
    older = exchange(sends)
    current, *sends = call(
        functools.partial(next_kernel, groups, block, 1),
        [whole] + [piece(2)] * groups, (place, picks), (driven, matrix, aside, *older, later[0], second),
    )
    found.append(current)
    pair = spread_tree(jnp.concatenate(found))
    blocks = exchange(sends)
    current, own, *sends = call(
        functools.partial(next_kernel, groups, block, 2),
        [whole, whole] + [piece()] * groups, (place, picks), (driven, matrix, aside, *blocks, *older, later[1]),
    )
    found.append(current)
    third = spread_tree(current)
    older = blocks
    from_second = along(own, [(2, 0)])
    blocks = exchange(sends)
    (current,) = call(
        functools.partial(next_kernel, groups, block, 3),
        [whole], (place, picks), (driven, matrix, aside, *blocks, *older, later[2], from_second),
    )
    copies = [along(current, [(0, 2 * z)]) for z in range(1, chips)]
    early = jnp.concatenate([pair, third])
    early = jnp.where(delay_index % 2 == 0, early, swap(early))
    far = functools.reduce(lambda a, b: a + b, copies)
    held = jnp.where(delay_index == 0, current, far)
    last = jnp.where(delay_index % 2 == 0, held, swap(held))
    return jnp.concatenate([early, last]).reshape(STEPS, rows, columns)


def solution(mesh):
    placed = (
        P("delay", "group", None, None, None),
        P("delay", "group", None),
        P("delay", "group"),
        P("delay", None, None),
        P("delay", "group", None),
        P(None, "group", None),
        P("group", None),
        P("group"),
    )
    return jax.shard_map(
        local, mesh=mesh, in_specs=placed, out_specs=P(None, "group", None), check_vma=False
    )
```

```python
import functools

import jax
import jax.numpy as jnp
from jax import lax
from jax.experimental import pallas as pl
from jax.experimental.pallas import tpu as pltpu
from jax.sharding import PartitionSpec as P


STEPS = 4

F32 = jnp.float32
BF16 = jnp.bfloat16
VMEM = pl.BlockSpec(memory_space=pltpu.VMEM)
SMEM = pl.BlockSpec(memory_space=pltpu.SMEM)


def peer_of(group, hop, groups):
    return group ^ hop if groups & (groups - 1) == 0 else (group + hop) % groups


def source_of(group, hop, groups):
    return group ^ hop if groups & (groups - 1) == 0 else (group - hop) % groups


def call(kernel, out_shape, scalars, arrays, spare=2):
    held = sum(a.size * a.dtype.itemsize for a in (*arrays, *jax.tree.leaves(out_shape)))
    return pl.pallas_call(
        kernel,
        out_shape=out_shape,
        in_specs=[SMEM] * len(scalars) + [VMEM] * len(arrays),
        out_specs=jax.tree.map(lambda _: VMEM, out_shape),
        compiler_params=pltpu.CompilerParams(vmem_limit_bytes=held + spare * (1 << 20)),
    )(*scalars, *arrays)


def dot(a, b):
    return jnp.dot(a, b, preferred_element_type=F32)


def dense_kernel(groups, block, depth, place, rows, counts, weights, dense):
    me = place[0]
    dense[...] = jnp.zeros_like(dense)
    for hop in range(groups):
        source = source_of(me, hop, groups)
        for entry in range(depth):

            @pl.when(entry < counts[0, source])
            def _():
                start = pl.multiple_of(rows[source, entry] * block, block)
                dense[pl.ds(start, block), hop * block : (hop + 1) * block] = weights[source, entry]


def sheet_kernel(self_block, column, row, sheet):
    scaled = self_block[...].astype(F32) * column[...]
    first = scaled.astype(BF16)
    second = dot(first, first)
    total = second - scaled
    third = dot(second.astype(BF16), first)
    sheet[...] = ((total - third) * row[...]).astype(BF16)


def product(matrix, blocks, part, block):
    total = None
    for hop, ref in enumerate(blocks):
        term = dot(matrix[:, hop * block : (hop + 1) * block], ref[part * block : (part + 1) * block, :])
        total = term if total is None else total + term
    return total


def emit(block, sends, part, sources, picks, row):
    for hop, out in enumerate(sends):
        start = pl.multiple_of(picks[row, hop] * block, block)
        out[part * block : (part + 1) * block, :] = sources[pl.ds(start, block), :]


def pick_kernel(block, parts, picks, *refs):
    sources, sends = refs[:parts], refs[parts:]
    for part, source in enumerate(sources):
        for hop, out in enumerate(sends):
            start = pl.multiple_of(picks[hop] * block, block)
            out[part * block : (part + 1) * block, :] = source[pl.ds(start, block), :]


def early_kernel(groups, block, place, matrix, *refs):
    blocks, outs = refs[:groups], refs[groups:]
    for part, out in enumerate(outs):

        @pl.when(place[1] >= part)
        def _():
            out[...] = product(matrix, blocks, part, block).astype(BF16)

        @pl.when(place[1] < part)
        def _():
            out[...] = jnp.zeros_like(out)


def near_kernel(groups, block, place, matrix, aside, *refs):
    blocks, refs = refs[:groups], refs[groups:]
    older, refs = (refs[:groups], refs[groups:]) if len(refs) > 2 else (None, refs)
    wide, narrow = refs
    total = product(matrix, blocks, 0, block)
    narrow[...] = jnp.where(place[1] >= 2, total, 0.0).astype(BF16)
    if older is not None:
        total = total + product(aside, older, 1, block)
    wide[...] = total


def step_kernel(block, step, fields, place, picks, sheet, column, incident, *refs):
    refs = list(refs)
    take = lambda count: [refs.pop(0) for _ in range(count)]
    terms = take(fields)
    wide = take(1)[0] if step > 0 else None
    history = take(1)[0] if step < 2 else None
    passed = take(1)[0] if step == 1 else None
    now, sends = refs[0], refs[1:]
    driving = incident[step].astype(F32)
    for ref in terms:
        driving = driving - ref[...].astype(F32)
    if wide is not None:
        driving = driving - wide[...]
    current = driving * column[...] + dot(sheet[...], driving.astype(BF16))
    now[...] = current.astype(BF16)
    if history is None:
        emit(block, sends, 0, now, picks, 0)
        return

    @pl.when(place[1] == 0)
    def _():
        emit(block, sends, 0, now, picks, 0)
        emit(block, sends, 1, now, picks, 1)

    inner = place[1] == 2 if passed is not None else False

    @pl.when((place[1] != 0) & jnp.logical_not(inner))
    def _():
        emit(block, sends, 0, history, picks, 0)
        emit(block, sends, 1, history, picks, 0)

    if passed is not None:

        @pl.when(inner)
        def _():
            emit(block, sends, 0, passed, picks, 0)
            emit(block, sends, 1, passed, picks, 0)


def last_kernel(groups, block, step, fields, sheet, column, incident, matrix, aside, *refs):
    blocks, older = refs[:groups], refs[groups : 2 * groups]
    terms, now = refs[2 * groups : 2 * groups + fields], refs[-1]
    driving = incident[step].astype(F32)
    for ref in terms:
        driving = driving - ref[...].astype(F32)
    driving = driving - product(matrix, blocks, 0, block) - product(aside, older, 1, block)
    now[...] = (driving * column[...] + dot(sheet[...], driving.astype(BF16))).astype(BF16)


def local(retarded, block_row, block_count, send_pick, history, incident, self_block, sheet_diag):
    groups = lax.axis_size("group")
    delays = lax.axis_size("delay")
    chips = delays // 2
    group_index = lax.axis_index("group")
    delay_index = lax.axis_index("delay")
    weights = retarded[0]
    depth, block = weights.shape[1], weights.shape[-1]
    rows, columns = history.shape[1:]
    shape = jax.ShapeDtypeStruct
    piece = lambda parts=1: shape((parts * block, columns), BF16)
    whole = shape((rows, columns), BF16)

    def along(array, pairs):
        return lax.ppermute(array, "delay", pairs)

    def swap(array):
        return along(array, [(d, d ^ 1) for d in range(delays)])

    def shift(array):
        return along(array, [(d, (d + 1) % delays) for d in range(delays)])

    def exchange(sends):
        return [sends[0]] + [
            lax.ppermute(sends[hop], "group", [(g, peer_of(g, hop, groups)) for g in range(groups)])
            for hop in range(1, groups)
        ]

    def plus(a, b):
        return (a.astype(F32) + b.astype(F32)).astype(BF16)

    def gathered(term):
        chip = plus(term, swap(term))
        return [chip] + [along(chip, [(2 * z, 0)]) for z in range(1, chips)]

    def spread_tree(array):
        stride = 1
        while stride < chips:
            stride *= 2
        held = array
        z = delay_index // 2
        while stride > 1:
            stride //= 2
            pairs = [(2 * c, 2 * (c + stride)) for c in range(0, chips, 2 * stride) if c + stride < chips]
            got = along(held, pairs)
            held = jnp.where(z % (2 * stride) == stride, got, held)
        return held

    earlier = shift(history[0])
    place = jnp.stack([group_index, delay_index]).astype(jnp.int32)
    hops = jnp.stack([peer_of(group_index, hop, groups) for hop in range(groups)])
    mine = lax.dynamic_index_in_dim(send_pick[0], group_index, 0, keepdims=False)[hops]
    inverse = 1.0 / sheet_diag
    column, row = inverse[:, None], inverse[None, :]
    dense = call(
        functools.partial(dense_kernel, groups, block, depth),
        shape((rows, groups * block), BF16),
        (place, block_row[0], block_count), (weights,),
    )
    sheet = call(sheet_kernel, shape((rows, rows), BF16), (), (self_block, column, row), 8 + 12)

    sends = call(
        functools.partial(pick_kernel, block, 2), [piece(2)] * groups, (mine,), (history[0], earlier)
    )
    blocks = exchange(sends)
    earlier = shift(earlier)
    terms = call(
        functools.partial(early_kernel, groups, block), [whole, whole], (place,), (dense, *blocks)
    )
    picks = jnp.stack([mine, swap(mine)])
    fields = gathered(terms[0])
    later = gathered(terms[1])
    oldest = shift(earlier)
    aside = swap(dense)

    law = (sheet, column, incident)
    current, *sends = call(
        functools.partial(step_kernel, block, 0, chips),
        [whole] + [piece(2)] * groups, (place, picks), (*law, *fields, earlier),
    )
    found = [current]
    older = exchange(sends)
    second = along(current, [(0, 2)])
    wide, narrow = call(
        functools.partial(near_kernel, groups, block),
        [shape((rows, columns), F32), whole], (place,), (dense, aside, *older),
    )
    fields = gathered(narrow)
    current, *sends = call(
        functools.partial(step_kernel, block, 1, chips),
        [whole] + [piece(2)] * groups, (place, picks), (*law, *later, wide, oldest, second),
    )
    found.append(current)
    blocks = exchange(sends)
    pair = spread_tree(jnp.concatenate(found))
    wide, narrow = call(
        functools.partial(near_kernel, groups, block),
        [shape((rows, columns), F32), whole], (place,), (dense, aside, *blocks, *older),
    )
    later = gathered(narrow)
    current, *sends = call(
        functools.partial(step_kernel, block, 2, chips),
        [whole] + [piece()] * groups, (place, picks), (*law, *fields, wide),
    )
    found.append(current)
    older = blocks
    blocks = exchange(sends)
    third = spread_tree(current)
    current = call(
        functools.partial(last_kernel, groups, block, 3, chips),
        whole, (), (*law, dense, aside, *blocks, *older, *later),
    )
    copies = [along(current, [(0, 2 * z)]) for z in range(1, chips)]
    early = jnp.concatenate([pair, third])
    early = jnp.where(delay_index % 2 == 0, early, swap(early))
    far = functools.reduce(lambda a, b: a + b, copies)
    held = jnp.where(delay_index == 0, current, far)
    last = jnp.where(delay_index % 2 == 0, held, swap(held))
    return jnp.concatenate([early, last]).reshape(STEPS, rows, columns)


def solution(mesh):
    placed = (
        P("delay", "group", None, None, None),
        P("delay", "group", None),
        P("delay", "group"),
        P("delay", None, None),
        P("delay", "group", None),
        P(None, "group", None),
        P("group", None),
        P("group"),
    )

    return jax.shard_map(local, mesh=mesh, in_specs=placed, out_specs=P(None, "group", None), check_vma=False)
```

```python
import functools

import jax
import jax.numpy as jnp
from jax import lax
from jax.experimental import pallas as pl
from jax.experimental.pallas import tpu as pltpu
from jax.sharding import PartitionSpec as P


STEPS = 4

F32 = jnp.float32
BF16 = jnp.bfloat16
VMEM = pl.BlockSpec(memory_space=pltpu.VMEM)
SMEM = pl.BlockSpec(memory_space=pltpu.SMEM)


def peer_of(group, hop, groups):
    return group ^ hop if groups & (groups - 1) == 0 else (group + hop) % groups


def source_of(group, hop, groups):
    return group ^ hop if groups & (groups - 1) == 0 else (group - hop) % groups


def call(kernel, out_shape, scalars, arrays, spare=2):
    held = sum(a.size * a.dtype.itemsize for a in (*arrays, *jax.tree.leaves(out_shape)))
    return pl.pallas_call(
        kernel,
        out_shape=out_shape,
        in_specs=[SMEM] * len(scalars) + [VMEM] * len(arrays),
        out_specs=jax.tree.map(lambda _: VMEM, out_shape),
        compiler_params=pltpu.CompilerParams(vmem_limit_bytes=held + spare * (1 << 20)),
    )(*scalars, *arrays)


def dot(a, b):
    return jnp.dot(a, b, preferred_element_type=F32)


def dense_kernel(groups, block, depth, rows, counts, weights, dense):
    me = lax.axis_index("group")
    dense[...] = jnp.zeros_like(dense)
    for hop in range(groups):
        source = source_of(me, hop, groups)
        for entry in range(depth):

            @pl.when(entry < counts[0, source])
            def _():
                start = pl.multiple_of(rows[0, source, entry] * block, block)
                dense[pl.ds(start, block), hop * block : (hop + 1) * block] = weights[source, entry]


def sheet_kernel(self_block, column, row, sheet):
    scaled = self_block[...].astype(F32) * column[...]
    first = scaled.astype(BF16)
    second = dot(first, first)
    total = second - scaled
    third = dot(second.astype(BF16), first)
    sheet[...] = ((total - third) * row[...]).astype(BF16)


def product(matrix, blocks, part, block):
    total = None
    for hop, ref in enumerate(blocks):
        term = dot(matrix[:, hop * block : (hop + 1) * block], ref[part * block : (part + 1) * block, :])
        total = term if total is None else total + term
    return total


def emit(groups, block, sends, part, source, table):
    me = lax.axis_index("group")
    for hop, out in enumerate(sends):
        start = pl.multiple_of(table[0, me, peer_of(me, hop, groups)] * block, block)
        out[part * block : (part + 1) * block, :] = source[pl.ds(start, block), :]


def pick_kernel(groups, block, table, first, second, *sends):
    emit(groups, block, sends, 0, first, table)
    emit(groups, block, sends, 1, second, table)


def early_kernel(groups, block, matrix, *refs):
    blocks, outs = refs[:groups], refs[groups:]
    delay = lax.axis_index("delay")
    for part, out in enumerate(outs):

        @pl.when(delay >= part)
        def _():
            out[...] = product(matrix, blocks, part, block).astype(BF16)

        @pl.when(delay < part)
        def _():
            out[...] = jnp.zeros_like(out)


def plus_kernel(first, second, out):
    out[...] = (first[...].astype(F32) + second[...].astype(F32)).astype(BF16)


def near_kernel(groups, block, matrix, aside, *refs):
    blocks, refs = refs[:groups], refs[groups:]
    older, refs = (refs[:groups], refs[groups:]) if len(refs) > 2 else (None, refs)
    wide, narrow = refs
    total = product(matrix, blocks, 0, block)
    narrow[...] = jnp.where(lax.axis_index("delay") >= 2, total, 0.0).astype(BF16)
    if older is not None:
        total = total + product(aside, older, 1, block)
    wide[...] = total


def law_of(driving, sheet, column):
    return (driving * column[...] + dot(sheet[...], driving.astype(BF16))).astype(BF16)


def driving_of(incident, step, terms):
    driving = incident[step].astype(F32)
    for ref in terms:
        driving = driving - ref[...].astype(F32)
    return driving


def step_kernel(groups, block, step, fields, table, other, sheet, column, incident, *refs):
    terms, refs = refs[:fields], refs[fields:]
    delay = lax.axis_index("delay")
    history = passed = second = None
    if step < 2:
        history, refs = refs[0], refs[1:]
    if step == 1:
        second, refs = refs[0], refs[1:]
    if step > 0:
        passed, refs = refs[0], refs[1:]
    carry, sends = refs[0], refs[1:]
    current = law_of(driving_of(incident, step, terms), sheet, column)
    if step > 0:

        @pl.when(delay == 0)
        def _():
            carry[...] = current

        @pl.when(delay != 0)
        def _():
            carry[...] = passed[...]

    else:
        carry[...] = current
    if step == 2:
        emit(groups, block, sends, 0, carry, table)
        return

    @pl.when(delay == 0)
    def _():
        emit(groups, block, sends, 0, carry, table)
        emit(groups, block, sends, 1, carry, other)

    @pl.when((delay != 0) if step == 0 else (delay != 0) & (delay != 2))
    def _():
        emit(groups, block, sends, 0, history, table)
        emit(groups, block, sends, 1, history, table)

    if step == 1:

        @pl.when(delay == 2)
        def _():
            emit(groups, block, sends, 0, second, table)
            emit(groups, block, sends, 1, second, table)


def last_kernel(groups, block, step, sheet, column, incident, matrix, aside, *refs):
    blocks, older, refs = refs[:groups], refs[groups : 2 * groups], refs[2 * groups :]
    terms, passed, carry = refs[:-2], refs[-2], refs[-1]
    delay = lax.axis_index("delay")
    driving = driving_of(incident, step, terms)
    driving = driving - product(matrix, blocks, 0, block) - product(aside, older, 1, block)
    current = law_of(driving, sheet, column)

    @pl.when(delay == 0)
    def _():
        carry[...] = current

    @pl.when(delay != 0)
    def _():
        carry[...] = passed[...]


def choose_kernel(plan, *refs):
    sources, out = refs[:-1], refs[-1]
    rows = sources[0].shape[0]
    chip = lax.axis_index("delay") // 2
    for z, chosen in enumerate(plan):

        @pl.when(chip == z)
        def _():
            for place, index in enumerate(chosen):
                out[place * rows : (place + 1) * rows, :] = sources[index][...]


def out_kernel(early, early_other, late, late_other, out, sems):
    split = early.shape[0]

    def write(first, second):
        copies = (
            pltpu.make_async_copy(first, out.at[:split], sems.at[0]),
            pltpu.make_async_copy(second, out.at[split:], sems.at[1]),
        )
        for copy in copies:
            copy.start()
        for copy in copies:
            copy.wait()

    odd = lax.axis_index("delay") % 2

    @pl.when(odd == 0)
    def _():
        write(early, late)

    @pl.when(odd == 1)
    def _():
        write(early_other, late_other)


def local(retarded, block_row, block_count, send_pick, history, incident, self_block, sheet_diag):
    groups = lax.axis_size("group")
    delays = lax.axis_size("delay")
    chips = delays // 2
    weights = retarded[0]
    depth, block = weights.shape[1], weights.shape[-1]
    rows, columns = history.shape[1:]
    shape = jax.ShapeDtypeStruct
    piece = lambda parts=1: shape((parts * block, columns), BF16)
    whole = shape((rows, columns), BF16)
    wide_whole = shape((rows, columns), F32)
    bind = functools.partial

    def along(array, pairs):
        return lax.ppermute(array, "delay", pairs)

    def swap(array):
        return along(array, [(d, d ^ 1) for d in range(delays)])

    def shift(array, by=1):
        return along(array, [(d, (d + by) % delays) for d in range(delays)])

    def exchange(sends):
        return [sends[0]] + [
            lax.ppermute(sends[hop], "group", [(g, peer_of(g, hop, groups)) for g in range(groups)])
            for hop in range(1, groups)
        ]

    def gathered(term):
        other = swap(term)
        chip = call(plus_kernel, whole, (), (term, other))
        return [chip] + [along(chip, [(2 * z, 0)]) for z in range(1, chips)]

    earlier = shift(history[0])
    other = swap(send_pick)
    inverse = 1.0 / sheet_diag
    column, row = inverse[:, None], inverse[None, :]
    dense = call(
        bind(dense_kernel, groups, block, depth),
        shape((rows, groups * block), BF16), (block_row, block_count), (weights,),
    )
    sheet = call(sheet_kernel, shape((rows, rows), BF16), (), (self_block, column, row), 20)

    sends = call(
        bind(pick_kernel, groups, block), [piece(2)] * groups, (send_pick,), (history[0], earlier)
    )
    blocks = exchange(sends)
    earlier = shift(earlier)
    terms = call(bind(early_kernel, groups, block), [whole, whole], (), (dense, *blocks))
    fields = gathered(terms[0])
    later = gathered(terms[1])
    oldest = shift(earlier)
    aside = swap(dense)

    law = (sheet, column, incident)
    tables = (send_pick, other)
    found, slots = [], []

    def stepped(step, fields, extra, parts):
        carry, *sends = call(
            bind(step_kernel, groups, block, step, len(fields)),
            [whole] + [piece(parts)] * groups, tables, (*law, *fields, *extra),
        )
        found.append(carry)
        return sends

    def rotate(array):
        slots.append(shift(array, 2))

    sends = stepped(0, fields, (earlier,), 2)
    older = exchange(sends)
    rotate(found[0])
    wide, narrow = call(
        bind(near_kernel, groups, block), [wide_whole, whole], (), (dense, aside, *older)
    )
    fields = gathered(narrow)
    sends = stepped(1, (*later, wide), (oldest, slots[0], slots[-1]), 2)
    blocks = exchange(sends)
    rotate(found[1])
    wide, narrow = call(
        bind(near_kernel, groups, block), [wide_whole, whole], (), (dense, aside, *blocks, *older)
    )
    later = gathered(narrow)
    sends = stepped(2, (*fields, wide), (slots[-1],), 1)
    older = blocks
    blocks = exchange(sends)
    rotate(found[2])
    carry = call(
        bind(last_kernel, groups, block, 3),
        whole, (), (*law, dense, aside, *blocks, *older, *later, slots[-1]),
    )
    found.append(carry)
    heads = [z for z in range(STEPS) if z < chips]
    finals = [
        along(carry, [(2 * z, 2 * (z + k)) for z in heads if z + k < chips]) for k in range(1, chips)
    ]

    def origin(step, z):
        beyond = z - (STEPS - 1 - step)
        if z == 0:
            return found[step]
        return finals[beyond - 1] if beyond > 0 else slots[step + z - 1]

    def chosen(steps):
        sources, plan = [], []
        for z in range(chips):
            plan.append([])
            for step in steps:
                array = origin(step, z)
                known = [k for k, source in enumerate(sources) if source is array]
                if not known:
                    sources.append(array)
                plan[-1].append(known[0] if known else len(sources) - 1)
        return call(
            bind(choose_kernel, plan), shape((len(steps) * rows, columns), BF16), (), sources
        )

    ready = [s for s in range(STEPS) if chips - 1 <= STEPS - 1 - s] or [0]
    early = chosen(ready)
    early_other = swap(early)
    late = chosen([s for s in range(STEPS) if s not in ready])
    late_other = swap(late)
    out = pl.pallas_call(
        out_kernel,
        out_shape=shape((STEPS * rows, columns), BF16),
        in_specs=[VMEM] * 4,
        out_specs=pl.BlockSpec(memory_space=pl.ANY),
        scratch_shapes=[pltpu.SemaphoreType.DMA((2,))],
        compiler_params=pltpu.CompilerParams(vmem_limit_bytes=4 << 20),
    )(early, early_other, late, late_other)
    return out.reshape(STEPS, rows, columns)


def solution(mesh):
    placed = (
        P("delay", "group", None, None, None),
        P("delay", "group", None),
        P("delay", "group"),
        P("delay", None, None),
        P("delay", "group", None),
        P(None, "group", None),
        P("group", None),
        P("group"),
    )

    return jax.shard_map(local, mesh=mesh, in_specs=placed, out_specs=P(None, "group", None), check_vma=False)
```

```python
import functools

import jax
import jax.numpy as jnp
from jax import lax
from jax.experimental import pallas as pl
from jax.experimental.pallas import tpu as pltpu
from jax.sharding import PartitionSpec as P


STEPS = 4

F32 = jnp.float32
BF16 = jnp.bfloat16
VMEM = pl.BlockSpec(memory_space=pltpu.VMEM)
SMEM = pl.BlockSpec(memory_space=pltpu.SMEM)


def peer_of(group, hop, groups):
    return group ^ hop if groups & (groups - 1) == 0 else (group + hop) % groups


def source_of(group, hop, groups):
    return group ^ hop if groups & (groups - 1) == 0 else (group - hop) % groups


def call(kernel, out_shape, scalars, arrays, spare=2):
    held = sum(a.size * a.dtype.itemsize for a in (*arrays, *jax.tree.leaves(out_shape)))
    return pl.pallas_call(
        kernel,
        out_shape=out_shape,
        in_specs=[SMEM] * len(scalars) + [VMEM] * len(arrays),
        out_specs=jax.tree.map(lambda _: VMEM, out_shape),
        compiler_params=pltpu.CompilerParams(vmem_limit_bytes=held + spare * (1 << 20)),
    )(*scalars, *arrays)


def dot(a, b):
    return jnp.dot(a, b, preferred_element_type=F32)


def dense_kernel(groups, block, depth, rows, counts, weights, dense):
    me = lax.axis_index("group")
    dense[...] = jnp.zeros_like(dense)
    for hop in range(groups):
        source = source_of(me, hop, groups)
        for entry in range(depth):

            @pl.when(entry < counts[0, source])
            def _():
                start = pl.multiple_of(rows[0, source, entry] * block, block)
                dense[pl.ds(start, block), hop * block : (hop + 1) * block] = weights[source, entry]


def sheet_kernel(self_block, column, row, sheet):
    scaled = self_block[...].astype(F32) * column[...]
    first = scaled.astype(BF16)
    second = dot(first, first)
    total = second - scaled
    third = dot(second.astype(BF16), first)
    sheet[...] = ((total - third) * row[...]).astype(BF16)


def product(matrix, blocks, part, block):
    total = None
    for hop, ref in enumerate(blocks):
        term = dot(matrix[:, hop * block : (hop + 1) * block], ref[part * block : (part + 1) * block, :])
        total = term if total is None else total + term
    return total


def emit(groups, block, sends, part, source, table):
    me = lax.axis_index("group")
    for hop, out in enumerate(sends):
        start = pl.multiple_of(table[0, me, peer_of(me, hop, groups)] * block, block)
        out[part * block : (part + 1) * block, :] = source[pl.ds(start, block), :]


def pick_kernel(groups, block, table, first, second, *sends):
    emit(groups, block, sends, 0, first, table)
    emit(groups, block, sends, 1, second, table)


def early_kernel(groups, block, matrix, *refs):
    blocks, outs = refs[:groups], refs[groups:]
    delay = lax.axis_index("delay")
    for part, out in enumerate(outs):

        @pl.when(delay >= part)
        def _():
            out[...] = product(matrix, blocks, part, block).astype(BF16)

        @pl.when(delay < part)
        def _():
            out[...] = jnp.zeros_like(out)


def plus_kernel(first, second, out):
    out[...] = (first[...].astype(F32) + second[...].astype(F32)).astype(BF16)


def near_kernel(groups, block, matrix, aside, *refs):
    blocks, refs = refs[:groups], refs[groups:]
    older, refs = (refs[:groups], refs[groups:]) if len(refs) > 2 else (None, refs)
    wide, narrow = refs
    total = product(matrix, blocks, 0, block)
    narrow[...] = jnp.where(lax.axis_index("delay") >= 2, total, 0.0).astype(BF16)
    if older is not None:
        total = total + product(aside, older, 1, block)
    wide[...] = total


def law_of(driving, sheet, column):
    return (driving * column[...] + dot(sheet[...], driving.astype(BF16))).astype(BF16)


def driving_of(incident, step, terms):
    driving = incident[step].astype(F32)
    for ref in terms:
        driving = driving - ref[...].astype(F32)
    return driving


def step_kernel(groups, block, step, fields, table, other, sheet, column, incident, *refs):
    terms, refs = refs[:fields], refs[fields:]
    delay = lax.axis_index("delay")
    history = passed = second = None
    if step < 2:
        history, refs = refs[0], refs[1:]
    if step == 1:
        second, refs = refs[0], refs[1:]
    if step > 0:
        passed, refs = refs[0], refs[1:]
    carry, sends = refs[0], refs[1:]
    current = law_of(driving_of(incident, step, terms), sheet, column)
    if step > 0:

        @pl.when(delay == 0)
        def _():
            carry[...] = current

        @pl.when(delay != 0)
        def _():
            carry[...] = passed[...]

    else:
        carry[...] = current
    if step == 2:
        emit(groups, block, sends, 0, carry, table)
        return

    @pl.when(delay == 0)
    def _():
        emit(groups, block, sends, 0, carry, table)
        emit(groups, block, sends, 1, carry, other)

    @pl.when((delay != 0) if step == 0 else (delay != 0) & (delay != 2))
    def _():
        emit(groups, block, sends, 0, history, table)
        emit(groups, block, sends, 1, history, table)

    if step == 1:

        @pl.when(delay == 2)
        def _():
            emit(groups, block, sends, 0, second, table)
            emit(groups, block, sends, 1, second, table)


def last_kernel(groups, block, step, sheet, column, incident, matrix, aside, *refs):
    blocks, older, refs = refs[:groups], refs[groups : 2 * groups], refs[2 * groups :]
    terms, passed, carry = refs[:-2], refs[-2], refs[-1]
    delay = lax.axis_index("delay")
    driving = driving_of(incident, step, terms)
    driving = driving - product(matrix, blocks, 0, block) - product(aside, older, 1, block)
    current = law_of(driving, sheet, column)

    @pl.when(delay == 0)
    def _():
        carry[...] = current

    @pl.when(delay != 0)
    def _():
        carry[...] = passed[...]


def choose_kernel(plan, *refs):
    sources, out = refs[:-1], refs[-1]
    rows = sources[0].shape[0]
    chip = lax.axis_index("delay") // 2
    for z, chosen in enumerate(plan):

        @pl.when(chip == z)
        def _():
            for place, index in enumerate(chosen):
                out[place * rows : (place + 1) * rows, :] = sources[index][...]


def out_kernel(early, early_other, late, late_other, out, sems):
    split = early.shape[0]

    def write(first, second):
        copies = (
            pltpu.make_async_copy(first, out.at[:split], sems.at[0]),
            pltpu.make_async_copy(second, out.at[split:], sems.at[1]),
        )
        for copy in copies:
            copy.start()
        for copy in copies:
            copy.wait()

    odd = lax.axis_index("delay") % 2

    @pl.when(odd == 0)
    def _():
        write(early, late)

    @pl.when(odd == 1)
    def _():
        write(early_other, late_other)


def local(retarded, block_row, block_count, send_pick, history, incident, self_block, sheet_diag):
    groups = lax.axis_size("group")
    delays = lax.axis_size("delay")
    chips = delays // 2
    weights = retarded[0]
    depth, block = weights.shape[1], weights.shape[-1]
    rows, columns = history.shape[1:]
    shape = jax.ShapeDtypeStruct
    piece = lambda parts=1: shape((parts * block, columns), BF16)
    whole = shape((rows, columns), BF16)
    wide_whole = shape((rows, columns), F32)
    bind = functools.partial

    def along(array, pairs):
        return lax.ppermute(array, "delay", pairs)

    def swap(array):
        return along(array, [(d, d ^ 1) for d in range(delays)])

    def shift(array, by=1):
        return along(array, [(d, (d + by) % delays) for d in range(delays)])

    def onward(array, by=1):
        return along(array, [(d, d + by) for d in range(0, delays - by, by)])

    def exchange(sends):
        return [sends[0]] + [
            lax.ppermute(sends[hop], "group", [(g, peer_of(g, hop, groups)) for g in range(groups)])
            for hop in range(1, groups)
        ]

    def gathered(term):
        other = swap(term)
        chip = call(plus_kernel, whole, (), (term, other))
        return [chip] + [along(chip, [(2 * z, 0)]) for z in range(1, chips)]

    earlier = shift(history[0])
    inverse = 1.0 / sheet_diag
    column, row = inverse[:, None], inverse[None, :]
    listed = jnp.clip(block_row, 0, rows // block - 1)
    dense = call(
        bind(dense_kernel, groups, block, depth),
        shape((rows, groups * block), BF16), (listed, block_count), (weights,),
    )
    sheet = call(sheet_kernel, shape((rows, rows), BF16), (), (self_block, column, row), 20)

    sends = call(
        bind(pick_kernel, groups, block), [piece(2)] * groups, (send_pick,), (history[0], earlier)
    )
    blocks = exchange(sends)
    earlier = shift(earlier)
    other = swap(send_pick)
    terms = call(bind(early_kernel, groups, block), [whole, whole], (), (dense, *blocks))
    fields = gathered(terms[0])
    later = gathered(terms[1])
    oldest = onward(earlier)
    aside = swap(dense)

    law = (sheet, column, incident)
    tables = (send_pick, other)
    found, slots = [], []

    def stepped(step, fields, extra, parts):
        carry, *sends = call(
            bind(step_kernel, groups, block, step, len(fields)),
            [whole] + [piece(parts)] * groups, tables, (*law, *fields, *extra),
        )
        found.append(carry)
        return sends

    def rotate(array):
        slots.append(onward(array, 2))

    sends = stepped(0, fields, (earlier,), 2)
    older = exchange(sends)
    rotate(found[0])
    wide, narrow = call(
        bind(near_kernel, groups, block), [wide_whole, whole], (), (dense, aside, *older)
    )
    fields = gathered(narrow)
    sends = stepped(1, (*later, wide), (oldest, slots[0], slots[-1]), 2)
    blocks = exchange(sends)
    rotate(found[1])
    wide, narrow = call(
        bind(near_kernel, groups, block), [wide_whole, whole], (), (dense, aside, *blocks, *older)
    )
    later = gathered(narrow)
    sends = stepped(2, (*fields, wide), (slots[-1],), 1)
    older = blocks
    blocks = exchange(sends)
    rotate(found[2])
    rotate(slots[-1])
    carry = call(
        bind(last_kernel, groups, block, 3),
        whole, (), (*law, dense, aside, *blocks, *older, *later, slots[-1]),
    )
    found.append(carry)
    reach = [STEPS - step for step in range(STEPS - 1)] + [0]
    heads = [z for z in reach if z < chips]
    finals = [
        along(carry, [(2 * z, 2 * (z + k)) for z in heads if z + k < chips]) for k in range(1, chips)
    ]

    def origin(step, z):
        beyond = z - reach[step]
        if z == 0:
            return found[step]
        return finals[beyond - 1] if beyond > 0 else slots[step + z - 1]

    def chosen(steps):
        sources, plan = [], []
        for z in range(chips):
            plan.append([])
            for step in steps:
                array = origin(step, z)
                known = [k for k, source in enumerate(sources) if source is array]
                if not known:
                    sources.append(array)
                plan[-1].append(known[0] if known else len(sources) - 1)
        return call(
            bind(choose_kernel, plan), shape((len(steps) * rows, columns), BF16), (), sources
        )

    ready = [s for s in range(STEPS) if chips - 1 <= reach[s]] or [0]
    early = chosen(ready)
    early_other = swap(early)
    late = chosen([s for s in range(STEPS) if s not in ready])
    late_other = swap(late)
    out = pl.pallas_call(
        out_kernel,
        out_shape=shape((STEPS * rows, columns), BF16),
        in_specs=[VMEM] * 4,
        out_specs=pl.BlockSpec(memory_space=pl.ANY),
        scratch_shapes=[pltpu.SemaphoreType.DMA((2,))],
        compiler_params=pltpu.CompilerParams(vmem_limit_bytes=4 << 20),
    )(early, early_other, late, late_other)
    return out.reshape(STEPS, rows, columns)


def solution(mesh):
    placed = (
        P("delay", "group", None, None, None),
        P("delay", "group", None),
        P("delay", "group"),
        P("delay", None, None),
        P("delay", "group", None),
        P(None, "group", None),
        P("group", None),
        P("group"),
    )

    return jax.shard_map(local, mesh=mesh, in_specs=placed, out_specs=P(None, "group", None), check_vma=False)
```

```python
import functools

import jax
import jax.numpy as jnp
from jax import lax
from jax.experimental import pallas as pl
from jax.experimental.pallas import tpu as pltpu
from jax.sharding import PartitionSpec as P


STEPS = 4

F32 = jnp.float32
BF16 = jnp.bfloat16
VMEM = pl.BlockSpec(memory_space=pltpu.VMEM)
SMEM = pl.BlockSpec(memory_space=pltpu.SMEM)


def peer_of(group, hop, groups):
    return group ^ hop if groups & (groups - 1) == 0 else (group + hop) % groups


def source_of(group, hop, groups):
    return group ^ hop if groups & (groups - 1) == 0 else (group - hop) % groups


def call(kernel, out_shape, scalars, arrays, spare=2):
    held = sum(a.size * a.dtype.itemsize for a in (*arrays, *jax.tree.leaves(out_shape)))
    return pl.pallas_call(
        kernel,
        out_shape=out_shape,
        in_specs=[SMEM] * len(scalars) + [VMEM] * len(arrays),
        out_specs=jax.tree.map(lambda _: VMEM, out_shape),
        compiler_params=pltpu.CompilerParams(vmem_limit_bytes=held + spare * (1 << 20)),
    )(*scalars, *arrays)


def dot(a, b):
    return jnp.dot(a, b, preferred_element_type=F32)


def dense_kernel(groups, block, depth, rows, counts, weights, dense):
    me = lax.axis_index("group")
    dense[...] = jnp.zeros_like(dense)
    for hop in range(groups):
        source = source_of(me, hop, groups)
        for entry in range(depth):

            @pl.when(entry < counts[0, source])
            def _():
                start = pl.multiple_of(rows[0, source, entry] * block, block)
                dense[pl.ds(start, block), hop * block : (hop + 1) * block] = weights[source, entry]


def sheet_kernel(self_block, column, row, sheet):
    scaled = self_block[...].astype(F32) * column[...]
    first = scaled.astype(BF16)
    second = dot(first, first)
    total = second - scaled
    third = dot(second.astype(BF16), first)
    sheet[...] = ((total - third) * row[...]).astype(BF16)


def product(matrix, blocks, part, block):
    total = None
    for hop, ref in enumerate(blocks):
        term = dot(matrix[:, hop * block : (hop + 1) * block], ref[part * block : (part + 1) * block, :])
        total = term if total is None else total + term
    return total


def emit(groups, block, sends, part, source, table):
    me = lax.axis_index("group")
    for hop, out in enumerate(sends):
        start = pl.multiple_of(table[0, me, peer_of(me, hop, groups)] * block, block)
        out[part * block : (part + 1) * block, :] = source[pl.ds(start, block), :]


def pick_kernel(groups, block, table, source, *sends):
    emit(groups, block, sends, 0, source, table)


def term_kernel(groups, block, first, matrix, *refs):
    blocks, out = refs[:groups], refs[groups]
    total = product(matrix, blocks, 0, block)
    if first > 0:
        total = jnp.where(lax.axis_index("delay") >= first, total, 0.0)
    out[...] = total.astype(BF16)


def plus_kernel(first, second, out):
    out[...] = (first[...].astype(F32) + second[...].astype(F32)).astype(BF16)


def near_kernel(groups, block, matrix, aside, *refs):
    blocks, refs = refs[:groups], refs[groups:]
    older, refs = (refs[:groups], refs[groups:]) if len(refs) > 2 else (None, refs)
    wide, narrow = refs
    total = product(matrix, blocks, 0, block)
    narrow[...] = jnp.where(lax.axis_index("delay") >= 2, total, 0.0).astype(BF16)
    if older is not None:
        total = total + product(aside, older, 1, block)
    wide[...] = total


def law_of(driving, sheet, column):
    return (driving * column[...] + dot(sheet[...], driving.astype(BF16))).astype(BF16)


def driving_of(incident, step, terms):
    driving = incident[step].astype(F32)
    for ref in terms:
        driving = driving - ref[...].astype(F32)
    return driving


def step_kernel(groups, block, step, fields, table, other, sheet, column, incident, *refs):
    terms, refs = refs[:fields], refs[fields:]
    delay = lax.axis_index("delay")
    history = second = None
    if step < 2:
        history, refs = refs[0], refs[1:]
    if step == 1:
        second, refs = refs[0], refs[1:]
    now, sends = refs[0], refs[1:]
    now[...] = law_of(driving_of(incident, step, terms), sheet, column)
    if step == 2:
        emit(groups, block, sends, 0, now, table)
        return

    @pl.when(delay == 0)
    def _():
        emit(groups, block, sends, 0, now, table)
        emit(groups, block, sends, 1, now, other)

    @pl.when((delay != 0) if step == 0 else (delay != 0) & (delay != 2))
    def _():
        emit(groups, block, sends, 0, history, table)
        emit(groups, block, sends, 1, history, table)

    if step == 1:

        @pl.when(delay == 2)
        def _():
            emit(groups, block, sends, 0, second, table)
            emit(groups, block, sends, 1, second, table)


def carry_kernel(current, passed, carry):
    delay = lax.axis_index("delay")

    @pl.when(delay == 0)
    def _():
        carry[...] = current[...]

    @pl.when(delay != 0)
    def _():
        carry[...] = passed[...]


def last_kernel(groups, block, step, sheet, column, incident, matrix, aside, *refs):
    blocks, older, refs = refs[:groups], refs[groups : 2 * groups], refs[2 * groups :]
    terms, passed, carry = refs[:-2], refs[-2], refs[-1]
    delay = lax.axis_index("delay")
    driving = driving_of(incident, step, terms)
    driving = driving - product(matrix, blocks, 0, block) - product(aside, older, 1, block)
    current = law_of(driving, sheet, column)

    @pl.when(delay == 0)
    def _():
        carry[...] = current

    @pl.when(delay != 0)
    def _():
        carry[...] = passed[...]


def choose_kernel(plan, *refs):
    sources, out = refs[:-1], refs[-1]
    rows = sources[0].shape[0]
    chip = lax.axis_index("delay") // 2
    for z, chosen in enumerate(plan):

        @pl.when(chip == z)
        def _():
            for place, index in enumerate(chosen):
                out[place * rows : (place + 1) * rows, :] = sources[index][...]


def out_kernel(early, early_other, late, late_other, out, sems):
    split = early.shape[0]

    def write(first, second):
        copies = (
            pltpu.make_async_copy(first, out.at[:split], sems.at[0]),
            pltpu.make_async_copy(second, out.at[split:], sems.at[1]),
        )
        for copy in copies:
            copy.start()
        for copy in copies:
            copy.wait()

    odd = lax.axis_index("delay") % 2

    @pl.when(odd == 0)
    def _():
        write(early, late)

    @pl.when(odd == 1)
    def _():
        write(early_other, late_other)


def local(retarded, block_row, block_count, send_pick, history, incident, self_block, sheet_diag):
    groups = lax.axis_size("group")
    delays = lax.axis_size("delay")
    chips = delays // 2
    weights = retarded[0]
    depth, block = weights.shape[1], weights.shape[-1]
    rows, columns = history.shape[1:]
    shape = jax.ShapeDtypeStruct
    piece = lambda parts=1: shape((parts * block, columns), BF16)
    whole = shape((rows, columns), BF16)
    wide_whole = shape((rows, columns), F32)
    bind = functools.partial

    def along(array, pairs):
        return lax.ppermute(array, "delay", pairs)

    def swap(array):
        return along(array, [(d, d ^ 1) for d in range(delays)])

    def shift(array, by=1):
        return along(array, [(d, (d + by) % delays) for d in range(delays)])

    def onward(array, by=1):
        return along(array, [(d, d + by) for d in range(0, delays - by, by)])

    def exchange(sends):
        return [sends[0]] + [
            lax.ppermute(sends[hop], "group", [(g, peer_of(g, hop, groups)) for g in range(groups)])
            for hop in range(1, groups)
        ]

    def gathered(term):
        other = swap(term)
        chip = call(plus_kernel, whole, (), (term, other))
        return [chip] + [along(chip, [(2 * z, 0)]) for z in range(1, chips)]

    earlier = shift(history[0])
    listed = jnp.clip(block_row, 0, rows // block - 1)

    def picked(array):
        return call(bind(pick_kernel, groups, block), [piece()] * groups, (send_pick,), (array,))

    def term_of(blocks, first):
        return call(bind(term_kernel, groups, block, first), whole, (), (dense, *blocks))

    sends = picked(history[0])
    blocks = exchange(sends)
    dense = call(
        bind(dense_kernel, groups, block, depth),
        shape((rows, groups * block), BF16), (listed, block_count), (weights,),
    )
    fields = gathered(term_of(blocks, 0))
    sends = picked(earlier)
    blocks = exchange(sends)
    earlier = onward(earlier)
    inverse = 1.0 / sheet_diag
    column, row = inverse[:, None], inverse[None, :]
    sheet = call(sheet_kernel, shape((rows, rows), BF16), (), (self_block, column, row), 20)
    later = gathered(term_of(blocks, 1))
    other = swap(send_pick)
    oldest = onward(earlier)
    aside = swap(dense)

    law = (sheet, column, incident)
    tables = (send_pick, other)
    found, slots = [], []

    def stepped(step, fields, extra, parts):
        current, *sends = call(
            bind(step_kernel, groups, block, step, len(fields)),
            [whole] + [piece(parts)] * groups, tables, (*law, *fields, *extra),
        )
        found.append(current)
        return sends

    def pass_on():
        array = found[-1]
        if slots:
            array = call(carry_kernel, whole, (), (array, slots[-1]))
        slots.append(onward(array, 2))

    def near_of(blocks, older):
        return call(
            bind(near_kernel, groups, block), [wide_whole, whole], (), (dense, aside, *blocks, *older)
        )

    sends = stepped(0, fields, (earlier,), 2)
    older = exchange(sends)
    pass_on()
    wide, narrow = near_of(older, ())
    fields = gathered(narrow)
    sends = stepped(1, (*later, wide), (oldest, slots[0]), 2)
    blocks = exchange(sends)
    pass_on()
    wide, narrow = near_of(blocks, older)
    later = gathered(narrow)
    sends = stepped(2, (*fields, wide), (), 1)
    older = blocks
    blocks = exchange(sends)
    pass_on()
    carry = call(
        bind(last_kernel, groups, block, 3),
        whole, (), (*law, dense, aside, *blocks, *older, *later, slots[-1]),
    )
    found.append(carry)
    reach = [STEPS - 1 - step for step in range(STEPS)]
    heads = [z for z in reach if z < chips]
    finals = [
        along(carry, [(2 * z, 2 * (z + k)) for z in heads if z + k < chips]) for k in range(1, chips)
    ]

    def origin(step, z):
        beyond = z - reach[step]
        if z == 0:
            return found[step]
        return finals[beyond - 1] if beyond > 0 else slots[step + z - 1]

    def chosen(steps):
        sources, plan = [], []
        for z in range(chips):
            plan.append([])
            for step in steps:
                array = origin(step, z)
                known = [k for k, source in enumerate(sources) if source is array]
                if not known:
                    sources.append(array)
                plan[-1].append(known[0] if known else len(sources) - 1)
        return call(
            bind(choose_kernel, plan), shape((len(steps) * rows, columns), BF16), (), sources
        )

    ready = [s for s in range(STEPS) if chips - 1 <= reach[s]] or [0]
    early = chosen(ready)
    early_other = swap(early)
    late = chosen([s for s in range(STEPS) if s not in ready])
    late_other = swap(late)
    out = pl.pallas_call(
        out_kernel,
        out_shape=shape((STEPS * rows, columns), BF16),
        in_specs=[VMEM] * 4,
        out_specs=pl.BlockSpec(memory_space=pl.ANY),
        scratch_shapes=[pltpu.SemaphoreType.DMA((2,))],
        compiler_params=pltpu.CompilerParams(vmem_limit_bytes=4 << 20),
    )(early, early_other, late, late_other)
    return out.reshape(STEPS, rows, columns)


def solution(mesh):
    placed = (
        P("delay", "group", None, None, None),
        P("delay", "group", None),
        P("delay", "group"),
        P("delay", None, None),
        P("delay", "group", None),
        P(None, "group", None),
        P("group", None),
        P("group"),
    )

    return jax.shard_map(local, mesh=mesh, in_specs=placed, out_specs=P(None, "group", None), check_vma=False)
```

```python
import functools

import jax
import jax.numpy as jnp
from jax import lax
from jax.experimental import pallas as pl
from jax.experimental.pallas import tpu as pltpu
from jax.sharding import PartitionSpec as P


STEPS = 4

F32 = jnp.float32
BF16 = jnp.bfloat16
VMEM = pl.BlockSpec(memory_space=pltpu.VMEM)
SMEM = pl.BlockSpec(memory_space=pltpu.SMEM)


def peer_of(group, hop, groups):
    return group ^ hop if groups & (groups - 1) == 0 else (group + hop) % groups


def source_of(group, hop, groups):
    return group ^ hop if groups & (groups - 1) == 0 else (group - hop) % groups


def call(kernel, out_shape, scalars, arrays, spare=2):
    held = sum(a.size * a.dtype.itemsize for a in (*arrays, *jax.tree.leaves(out_shape)))
    return pl.pallas_call(
        kernel,
        out_shape=out_shape,
        in_specs=[SMEM] * len(scalars) + [VMEM] * len(arrays),
        out_specs=jax.tree.map(lambda _: VMEM, out_shape),
        compiler_params=pltpu.CompilerParams(vmem_limit_bytes=held + spare * (1 << 20)),
    )(*scalars, *arrays)


def dot(a, b):
    return jnp.dot(a, b, preferred_element_type=F32)


def dense_kernel(groups, block, depth, rows, counts, weights, dense):
    me = lax.axis_index("group")
    dense[...] = jnp.zeros_like(dense)
    for hop in range(groups):
        source = source_of(me, hop, groups)
        for entry in range(depth):

            @pl.when(entry < counts[0, source])
            def _():
                start = pl.multiple_of(rows[0, source, entry] * block, block)
                dense[pl.ds(start, block), hop * block : (hop + 1) * block] = weights[source, entry]


def sheet_kernel(self_block, column, row, sheet):
    scaled = self_block[...].astype(F32) * column[...]
    first = scaled.astype(BF16)
    second = dot(first, first)
    total = second - scaled
    third = dot(second.astype(BF16), first)
    sheet[...] = ((total - third) * row[...]).astype(BF16)


def product(matrix, blocks, part, block):
    total = None
    for hop, ref in enumerate(blocks):
        term = dot(matrix[:, hop * block : (hop + 1) * block], ref[part * block : (part + 1) * block, :])
        total = term if total is None else total + term
    return total


def emit(groups, block, sends, part, source, table):
    me = lax.axis_index("group")
    for hop, out in enumerate(sends):
        start = pl.multiple_of(table[0, me, peer_of(me, hop, groups)] * block, block)
        out[part * block : (part + 1) * block, :] = source[pl.ds(start, block), :]


def pick_kernel(groups, block, table, source, *sends):
    emit(groups, block, sends, 0, source, table)


def term_kernel(groups, block, first, matrix, *refs):
    blocks, out = refs[:groups], refs[groups]
    total = product(matrix, blocks, 0, block)
    if first > 0:
        total = jnp.where(lax.axis_index("delay") >= first, total, 0.0)
    out[...] = total.astype(BF16)


def plus_kernel(first, second, out):
    out[...] = (first[...].astype(F32) + second[...].astype(F32)).astype(BF16)


def near_kernel(groups, block, matrix, aside, *refs):
    blocks, refs = refs[:groups], refs[groups:]
    older, refs = (refs[:groups], refs[groups:]) if len(refs) > 2 else (None, refs)
    wide, narrow = refs
    total = product(matrix, blocks, 0, block)
    narrow[...] = jnp.where(lax.axis_index("delay") >= 2, total, 0.0).astype(BF16)
    if older is not None:
        total = total + product(aside, older, 1, block)
    wide[...] = total


def law_of(driving, sheet, column):
    return (driving * column[...] + dot(sheet[...], driving.astype(BF16))).astype(BF16)


def driving_of(incident, step, terms):
    driving = incident[step].astype(F32)
    for ref in terms:
        driving = driving - ref[...].astype(F32)
    return driving


def step_kernel(groups, block, step, fields, table, other, sheet, column, incident, *refs):
    terms, refs = refs[:fields], refs[fields:]
    delay = lax.axis_index("delay")
    history = second = None
    if step < 2:
        history, refs = refs[0], refs[1:]
    if step == 1:
        second, refs = refs[0], refs[1:]
    now, sends = refs[0], refs[1:]
    now[...] = law_of(driving_of(incident, step, terms), sheet, column)
    if step == 2:
        emit(groups, block, sends, 0, now, table)
        return

    @pl.when(delay == 0)
    def _():
        emit(groups, block, sends, 0, now, table)
        emit(groups, block, sends, 1, now, other)

    @pl.when((delay != 0) if step == 0 else (delay != 0) & (delay != 2))
    def _():
        emit(groups, block, sends, 0, history, table)
        emit(groups, block, sends, 1, history, table)

    if step == 1:

        @pl.when(delay == 2)
        def _():
            emit(groups, block, sends, 0, second, table)
            emit(groups, block, sends, 1, second, table)


def carry_kernel(current, passed, carry):
    delay = lax.axis_index("delay")

    @pl.when(delay == 0)
    def _():
        carry[...] = current[...]

    @pl.when(delay != 0)
    def _():
        carry[...] = passed[...]


def last_kernel(groups, block, step, sheet, column, incident, matrix, aside, *refs):
    blocks, older, refs = refs[:groups], refs[groups : 2 * groups], refs[2 * groups :]
    terms, now = refs[:-1], refs[-1]
    driving = driving_of(incident, step, terms)
    driving = driving - product(matrix, blocks, 0, block) - product(aside, older, 1, block)
    now[...] = law_of(driving, sheet, column)


def choose_kernel(plan, *refs):
    sources, out = refs[:-1], refs[-1]
    rows = sources[0].shape[0]
    chip = lax.axis_index("delay") // 2
    for z, chosen in enumerate(plan):

        @pl.when(chip == z)
        def _():
            for place, index in enumerate(chosen):
                out[place * rows : (place + 1) * rows, :] = sources[index][...]


def out_kernel(early, early_other, late, late_other, out, sems):
    split = early.shape[0]

    def write(first, second):
        copies = (
            pltpu.make_async_copy(first, out.at[:split], sems.at[0]),
            pltpu.make_async_copy(second, out.at[split:], sems.at[1]),
        )
        for copy in copies:
            copy.start()
        for copy in copies:
            copy.wait()

    odd = lax.axis_index("delay") % 2

    @pl.when(odd == 0)
    def _():
        write(early, late)

    @pl.when(odd == 1)
    def _():
        write(early_other, late_other)


def local(retarded, block_row, block_count, send_pick, history, incident, self_block, sheet_diag):
    groups = lax.axis_size("group")
    delays = lax.axis_size("delay")
    chips = delays // 2
    weights = retarded[0]
    depth, block = weights.shape[1], weights.shape[-1]
    rows, columns = history.shape[1:]
    shape = jax.ShapeDtypeStruct
    piece = lambda parts=1: shape((parts * block, columns), BF16)
    whole = shape((rows, columns), BF16)
    wide_whole = shape((rows, columns), F32)
    bind = functools.partial

    def along(array, pairs):
        return lax.ppermute(array, "delay", pairs)

    def swap(array):
        return along(array, [(d, d ^ 1) for d in range(delays)])

    def shift(array, by=1):
        return along(array, [(d, (d + by) % delays) for d in range(delays)])

    def onward(array, by=1):
        return along(array, [(d, d + by) for d in range(0, delays - by, by)])

    def exchange(sends):
        return [sends[0]] + [
            lax.ppermute(sends[hop], "group", [(g, peer_of(g, hop, groups)) for g in range(groups)])
            for hop in range(1, groups)
        ]

    def gathered(term):
        other = swap(term)
        chip = call(plus_kernel, whole, (), (term, other))
        return [chip] + [along(chip, [(2 * z, 0)]) for z in range(1, chips)]

    earlier = shift(history[0])
    listed = jnp.clip(block_row, 0, rows // block - 1)

    def picked(array):
        return call(bind(pick_kernel, groups, block), [piece()] * groups, (send_pick,), (array,))

    def term_of(blocks, first):
        return call(bind(term_kernel, groups, block, first), whole, (), (dense, *blocks))

    sends = picked(history[0])
    blocks = exchange(sends)
    dense = call(
        bind(dense_kernel, groups, block, depth),
        shape((rows, groups * block), BF16), (listed, block_count), (weights,),
    )
    fields = gathered(term_of(blocks, 0))
    sends = picked(earlier)
    blocks = exchange(sends)
    earlier = onward(earlier)
    inverse = 1.0 / sheet_diag
    column, row = inverse[:, None], inverse[None, :]
    sheet = call(sheet_kernel, shape((rows, rows), BF16), (), (self_block, column, row), 20)
    later = gathered(term_of(blocks, 1))
    other = swap(send_pick)
    oldest = onward(earlier)
    aside = swap(dense)

    law = (sheet, column, incident)
    tables = (send_pick, other)
    found, slots = [], []

    def stepped(step, fields, extra, parts):
        current, *sends = call(
            bind(step_kernel, groups, block, step, len(fields)),
            [whole] + [piece(parts)] * groups, tables, (*law, *fields, *extra),
        )
        found.append(current)
        return sends

    def pass_on():
        array = found[-1]
        if slots:
            array = call(carry_kernel, whole, (), (array, slots[-1]))
        slots.append(onward(array, 2))

    def near_of(blocks, older):
        return call(
            bind(near_kernel, groups, block), [wide_whole, whole], (), (dense, aside, *blocks, *older)
        )

    sends = stepped(0, fields, (earlier,), 2)
    older = exchange(sends)
    pass_on()
    wide, narrow = near_of(older, ())
    fields = gathered(narrow)
    sends = stepped(1, (*later, wide), (oldest, slots[0]), 2)
    blocks = exchange(sends)
    pass_on()
    wide, narrow = near_of(blocks, older)
    later = gathered(narrow)
    sends = stepped(2, (*fields, wide), (), 1)
    older = blocks
    blocks = exchange(sends)
    pass_on()
    found.append(
        call(
            bind(last_kernel, groups, block, 3), whole, (),
            (*law, dense, aside, *blocks, *older, *later),
        )
    )
    carry = call(carry_kernel, whole, (), (found[-1], slots[-1]))
    reach = [STEPS - 1 - step for step in range(STEPS)]
    heads = [z for z in reach if z < chips]
    finals = []
    for k in range(1, chips):
        pairs = [(2 * z, 2 * (z + k)) for z in heads if z + k < chips]
        finals.append(along(found[-1] if len(pairs) == 1 else carry, pairs))

    def origin(step, z):
        beyond = z - reach[step]
        if z == 0:
            return found[step]
        return finals[beyond - 1] if beyond > 0 else slots[step + z - 1]

    def chosen(steps):
        sources, plan = [], []
        for z in range(chips):
            plan.append([])
            for step in steps:
                array = origin(step, z)
                known = [k for k, source in enumerate(sources) if source is array]
                if not known:
                    sources.append(array)
                plan[-1].append(known[0] if known else len(sources) - 1)
        return call(
            bind(choose_kernel, plan), shape((len(steps) * rows, columns), BF16), (), sources
        )

    ready = [s for s in range(STEPS) if chips - 1 <= reach[s]] or [0]
    early = chosen(ready)
    early_other = swap(early)
    late = chosen([s for s in range(STEPS) if s not in ready])
    late_other = swap(late)
    out = pl.pallas_call(
        out_kernel,
        out_shape=shape((STEPS * rows, columns), BF16),
        in_specs=[VMEM] * 4,
        out_specs=pl.BlockSpec(memory_space=pl.ANY),
        scratch_shapes=[pltpu.SemaphoreType.DMA((2,))],
        compiler_params=pltpu.CompilerParams(vmem_limit_bytes=4 << 20),
    )(early, early_other, late, late_other)
    return out.reshape(STEPS, rows, columns)


def solution(mesh):
    placed = (
        P("delay", "group", None, None, None),
        P("delay", "group", None),
        P("delay", "group"),
        P("delay", None, None),
        P("delay", "group", None),
        P(None, "group", None),
        P("group", None),
        P("group"),
    )

    return jax.shard_map(local, mesh=mesh, in_specs=placed, out_specs=P(None, "group", None), check_vma=False)
```

```python
import functools

import jax
import jax.numpy as jnp
from jax import lax
from jax.experimental import pallas as pl
from jax.experimental.pallas import tpu as pltpu
from jax.sharding import PartitionSpec as P


STEPS = 4

F32 = jnp.float32
BF16 = jnp.bfloat16
VMEM = pl.BlockSpec(memory_space=pltpu.VMEM)
SMEM = pl.BlockSpec(memory_space=pltpu.SMEM)


def peer_of(group, hop, groups):
    return group ^ hop if groups & (groups - 1) == 0 else (group + hop) % groups


def source_of(group, hop, groups):
    return group ^ hop if groups & (groups - 1) == 0 else (group - hop) % groups


def call(kernel, out_shape, scalars, arrays, spare=2):
    held = sum(a.size * a.dtype.itemsize for a in (*arrays, *jax.tree.leaves(out_shape)))
    return pl.pallas_call(
        kernel,
        out_shape=out_shape,
        in_specs=[SMEM] * len(scalars) + [VMEM] * len(arrays),
        out_specs=jax.tree.map(lambda _: VMEM, out_shape),
        compiler_params=pltpu.CompilerParams(vmem_limit_bytes=held + spare * (1 << 20)),
    )(*scalars, *arrays)


def dot(a, b):
    return jnp.dot(a, b, preferred_element_type=F32)


def dense_kernel(groups, block, depth, rows, counts, weights, dense):
    me = lax.axis_index("group")
    dense[...] = jnp.zeros_like(dense)
    for hop in range(groups):
        source = source_of(me, hop, groups)
        for entry in range(depth):

            @pl.when(entry < counts[0, source])
            def _():
                start = pl.multiple_of(rows[0, source, entry] * block, block)
                dense[pl.ds(start, block), hop * block : (hop + 1) * block] = weights[source, entry]


def sheet_kernel(self_block, column, row, sheet):
    scaled = self_block[...].astype(F32) * column[...]
    first = scaled.astype(BF16)
    second = dot(first, first)
    total = second - scaled
    third = dot(second.astype(BF16), first)
    sheet[...] = ((total - third) * row[...]).astype(BF16)


def product(matrix, blocks, part, block):
    total = None
    for hop, ref in enumerate(blocks):
        term = dot(matrix[:, hop * block : (hop + 1) * block], ref[part * block : (part + 1) * block, :])
        total = term if total is None else total + term
    return total


def emit(groups, block, sends, part, source, table):
    me = lax.axis_index("group")
    for hop, out in enumerate(sends):
        start = pl.multiple_of(table[0, me, peer_of(me, hop, groups)] * block, block)
        out[part * block : (part + 1) * block, :] = source[pl.ds(start, block), :]


def pick_kernel(groups, block, table, source, *sends):
    emit(groups, block, sends, 0, source, table)


def term_kernel(groups, block, first, matrix, *refs):
    blocks, out = refs[:groups], refs[groups]
    total = product(matrix, blocks, 0, block)
    if first > 0:
        total = jnp.where(lax.axis_index("delay") >= first, total, 0.0)
    out[...] = total.astype(BF16)


def plus_kernel(start, first, second, out):
    total = first[...].astype(F32) + second[...].astype(F32)
    if start > 0:
        total = jnp.where(lax.axis_index("delay") >= start, total, 0.0)
    out[...] = total.astype(BF16)


def near_kernel(groups, block, first, matrix, *refs):
    blocks, wide, narrow = refs[:groups], refs[groups], refs[groups + 1]
    total = product(matrix, blocks, 0, block)
    narrow[...] = jnp.where(lax.axis_index("delay") >= first, total, 0.0).astype(BF16)
    wide[...] = total


def law_of(driving, sheet, column):
    return (driving * column[...] + dot(sheet[...], driving.astype(BF16))).astype(BF16)


def driving_of(incident, step, terms):
    driving = incident[step].astype(F32)
    for ref in terms:
        driving = driving - ref[...].astype(F32)
    return driving


def step_kernel(groups, block, step, fields, table, other, sheet, column, incident, *refs):
    terms, sources, refs = refs[:fields], refs[fields:-groups - 1], refs[-groups - 1 :]
    now, sends = refs[0], refs[1:]
    delay = lax.axis_index("delay")
    now[...] = law_of(driving_of(incident, step, terms), sheet, column)
    if step == 2:
        emit(groups, block, sends, 0, now, table)
        return

    @pl.when(delay == 0)
    def _():
        emit(groups, block, sends, 0, now, table)
        if step == 1:
            emit(groups, block, sends, 1, now, other)

    for place, source in enumerate(sources, 1):
        last = place == len(sources)

        @pl.when((delay >= place) if last else (delay == place))
        def _(source=source):
            emit(groups, block, sends, 0, source, table)
            if step == 1:
                emit(groups, block, sends, 1, source, table)


def carry_kernel(current, passed, carry):
    delay = lax.axis_index("delay")

    @pl.when(delay == 0)
    def _():
        carry[...] = current[...]

    @pl.when(delay != 0)
    def _():
        carry[...] = passed[...]


def last_kernel(groups, block, step, sheet, column, incident, matrix, aside, *refs):
    blocks, older, refs = refs[:groups], refs[groups : 2 * groups], refs[2 * groups :]
    terms, now = refs[:-1], refs[-1]
    driving = driving_of(incident, step, terms)
    driving = driving - product(matrix, blocks, 0, block) - product(aside, older, 1, block)
    now[...] = law_of(driving, sheet, column)


def choose_kernel(plan, *refs):
    sources, out = refs[:-1], refs[-1]
    rows = sources[0].shape[0]
    chip = lax.axis_index("delay") // 2
    for z, chosen in enumerate(plan):

        @pl.when(chip == z)
        def _():
            for place, index in enumerate(chosen):
                out[place * rows : (place + 1) * rows, :] = sources[index][...]


def out_kernel(early, early_other, late, late_other, out, sems):
    split = early.shape[0]

    def write(first, second):
        copies = (
            pltpu.make_async_copy(first, out.at[:split], sems.at[0]),
            pltpu.make_async_copy(second, out.at[split:], sems.at[1]),
        )
        for copy in copies:
            copy.start()
        for copy in copies:
            copy.wait()

    odd = lax.axis_index("delay") % 2

    @pl.when(odd == 0)
    def _():
        write(early, late)

    @pl.when(odd == 1)
    def _():
        write(early_other, late_other)


def local(retarded, block_row, block_count, send_pick, history, incident, self_block, sheet_diag):
    groups = lax.axis_size("group")
    delays = lax.axis_size("delay")
    chips = delays // 2
    weights = retarded[0]
    depth, block = weights.shape[1], weights.shape[-1]
    rows, columns = history.shape[1:]
    shape = jax.ShapeDtypeStruct
    piece = lambda parts=1: shape((parts * block, columns), BF16)
    whole = shape((rows, columns), BF16)
    wide_whole = shape((rows, columns), F32)
    bind = functools.partial

    def along(array, pairs):
        return lax.ppermute(array, "delay", pairs)

    def swap(array):
        return along(array, [(d, d ^ 1) for d in range(delays)])

    def shift(array, by=1):
        return along(array, [(d, (d + by) % delays) for d in range(delays)])

    def onward(array, by=1):
        return along(array, [(d, d + by) for d in range(0, delays - by, by)])

    def exchange(sends):
        return [sends[0]] + [
            lax.ppermute(sends[hop], "group", [(g, peer_of(g, hop, groups)) for g in range(groups)])
            for hop in range(1, groups)
        ]

    def gathered(term, first=0):
        other = swap(term)
        chip = call(bind(plus_kernel, first), whole, (), (term, other))
        fields = [chip]
        for z in range(1, chips):
            fields.append(along(chip, [(2 * z, 0)]))
        return fields, other

    earlier = shift(history[0])
    listed = jnp.clip(block_row, 0, rows // block - 1)

    def picked(array):
        return call(bind(pick_kernel, groups, block), [piece()] * groups, (send_pick,), (array,))

    def term_of(blocks, first):
        return call(bind(term_kernel, groups, block, first), whole, (), (dense, *blocks))

    sends = picked(history[0])
    blocks = exchange(sends)
    dense = call(
        bind(dense_kernel, groups, block, depth),
        shape((rows, groups * block), BF16), (listed, block_count), (weights,),
    )
    fields, _ = gathered(term_of(blocks, 0))
    sends = picked(earlier)
    blocks = exchange(sends)
    earlier = shift(earlier)
    inverse = 1.0 / sheet_diag
    column, row = inverse[:, None], inverse[None, :]
    sheet = call(sheet_kernel, shape((rows, rows), BF16), (), (self_block, column, row), 20)
    later, _ = gathered(term_of(blocks, 1))
    other = swap(send_pick)
    oldest = shift(earlier)
    aside = swap(dense)

    law = (sheet, column, incident)
    tables = (send_pick, other)
    found, slots = [], []

    def stepped(step, fields, extra, parts):
        current, *sends = call(
            bind(step_kernel, groups, block, step, len(fields)),
            [whole] + [piece(parts)] * groups, tables, (*law, *fields, *extra),
        )
        found.append(current)
        return sends

    def pass_on():
        array = found[-1]
        if slots:
            array = call(carry_kernel, whole, (), (array, slots[-1]))
        slots.append(onward(array, 2))

    def near_of(blocks, first):
        return call(
            bind(near_kernel, groups, block, first), [wide_whole, whole], (), (dense, *blocks)
        )

    sends = stepped(0, fields, (earlier,), 1)
    blocks = exchange(sends)
    handed = swap(found[0])
    pass_on()
    wide, narrow = near_of(blocks, 2)
    fields, _ = gathered(narrow)
    sends = stepped(1, (*later, wide), (handed, slots[0], oldest), 2)
    older = exchange(sends)
    pass_on()
    wide, narrow = near_of(older, 1)
    later, partner = gathered(narrow, 2)
    sends = stepped(2, (*fields, wide, partner), (), 1)
    blocks = exchange(sends)
    pass_on()
    found.append(
        call(
            bind(last_kernel, groups, block, 3), whole, (),
            (*law, dense, aside, *blocks, *older, *later),
        )
    )
    carry = call(carry_kernel, whole, (), (found[-1], slots[-1]))
    reach = [STEPS - 1 - step for step in range(STEPS)]
    heads = [z for z in reach if z < chips]
    finals = []
    for k in range(1, chips):
        pairs = [(2 * z, 2 * (z + k)) for z in heads if z + k < chips]
        finals.append(along(found[-1] if len(pairs) == 1 else carry, pairs))

    def origin(step, z):
        beyond = z - reach[step]
        if z == 0:
            return found[step]
        return finals[beyond - 1] if beyond > 0 else slots[step + z - 1]

    def chosen(steps):
        sources, plan = [], []
        for z in range(chips):
            plan.append([])
            for step in steps:
                array = origin(step, z)
                known = [k for k, source in enumerate(sources) if source is array]
                if not known:
                    sources.append(array)
                plan[-1].append(known[0] if known else len(sources) - 1)
        return call(
            bind(choose_kernel, plan), shape((len(steps) * rows, columns), BF16), (), sources
        )

    ready = [s for s in range(STEPS) if chips - 1 <= reach[s]] or [0]
    early = chosen(ready)
    early_other = swap(early)
    late = chosen([s for s in range(STEPS) if s not in ready])
    late_other = swap(late)
    out = pl.pallas_call(
        out_kernel,
        out_shape=shape((STEPS * rows, columns), BF16),
        in_specs=[VMEM] * 4,
        out_specs=pl.BlockSpec(memory_space=pl.ANY),
        scratch_shapes=[pltpu.SemaphoreType.DMA((2,))],
        compiler_params=pltpu.CompilerParams(vmem_limit_bytes=4 << 20),
    )(early, early_other, late, late_other)
    return out.reshape(STEPS, rows, columns)


def solution(mesh):
    placed = (
        P("delay", "group", None, None, None),
        P("delay", "group", None),
        P("delay", "group"),
        P("delay", None, None),
        P("delay", "group", None),
        P(None, "group", None),
        P("group", None),
        P("group"),
    )

    return jax.shard_map(local, mesh=mesh, in_specs=placed, out_specs=P(None, "group", None), check_vma=False)
```

```python
import functools

import jax
import jax.numpy as jnp
from jax import lax
from jax.experimental import pallas as pl
from jax.experimental.pallas import tpu as pltpu
from jax.sharding import PartitionSpec as P


STEPS = 4

F32 = jnp.float32
BF16 = jnp.bfloat16
VMEM = pl.BlockSpec(memory_space=pltpu.VMEM)
SMEM = pl.BlockSpec(memory_space=pltpu.SMEM)


def peer_of(group, hop, groups):
    return group ^ hop if groups & (groups - 1) == 0 else (group + hop) % groups


def source_of(group, hop, groups):
    return group ^ hop if groups & (groups - 1) == 0 else (group - hop) % groups


def call(kernel, out_shape, scalars, arrays, spare=2):
    held = sum(a.size * a.dtype.itemsize for a in (*arrays, *jax.tree.leaves(out_shape)))
    return pl.pallas_call(
        kernel,
        out_shape=out_shape,
        in_specs=[SMEM] * len(scalars) + [VMEM] * len(arrays),
        out_specs=jax.tree.map(lambda _: VMEM, out_shape),
        compiler_params=pltpu.CompilerParams(vmem_limit_bytes=held + spare * (1 << 20)),
    )(*scalars, *arrays)


def dot(a, b):
    return jnp.dot(a, b, preferred_element_type=F32)


def dense_kernel(groups, block, depth, rows, counts, weights, dense):
    me = lax.axis_index("group")
    dense[...] = jnp.zeros_like(dense)
    for hop in range(groups):
        source = source_of(me, hop, groups)
        for entry in range(depth):

            @pl.when(entry < counts[0, source])
            def _():
                start = pl.multiple_of(rows[0, source, entry] * block, block)
                dense[pl.ds(start, block), hop * block : (hop + 1) * block] = weights[source, entry]


def sheet_kernel(self_block, column, row, sheet):
    scaled = self_block[...].astype(F32) * column[...]
    first = scaled.astype(BF16)
    second = dot(first, first)
    total = second - scaled
    third = dot(second.astype(BF16), first)
    sheet[...] = ((total - third) * row[...]).astype(BF16)


def product(matrix, blocks, part, block):
    total = None
    for hop, ref in enumerate(blocks):
        term = dot(matrix[:, hop * block : (hop + 1) * block], ref[part * block : (part + 1) * block, :])
        total = term if total is None else total + term
    return total


def emit(groups, block, sends, part, source, table):
    me = lax.axis_index("group")
    for hop, out in enumerate(sends):
        start = pl.multiple_of(table[0, me, peer_of(me, hop, groups)] * block, block)
        out[part * block : (part + 1) * block, :] = source[pl.ds(start, block), :]


def pick_kernel(groups, block, table, source, *sends):
    emit(groups, block, sends, 0, source, table)


def term_kernel(groups, block, first, matrix, *refs):
    blocks, out = refs[:groups], refs[groups]
    total = product(matrix, blocks, 0, block)
    if first > 0:
        total = jnp.where(lax.axis_index("delay") >= first, total, 0.0)
    out[...] = total.astype(BF16)


def plus_kernel(start, first, second, out):
    total = first[...].astype(F32) + second[...].astype(F32)
    if start > 0:
        total = jnp.where(lax.axis_index("delay") >= start, total, 0.0)
    out[...] = total.astype(BF16)


def near_kernel(groups, block, first, matrix, *refs):
    blocks, wide, narrow = refs[:groups], refs[groups], refs[groups + 1]
    total = product(matrix, blocks, 0, block)
    narrow[...] = jnp.where(lax.axis_index("delay") >= first, total, 0.0).astype(BF16)
    wide[...] = total


def law_of(driving, sheet, column):
    return (driving * column[...] + dot(sheet[...], driving.astype(BF16))).astype(BF16)


def driving_of(incident, step, terms):
    driving = incident[step].astype(F32)
    for ref in terms:
        driving = driving - ref[...].astype(F32)
    return driving


def step_kernel(groups, block, step, fields, table, other, sheet, column, incident, *refs):
    terms, sources, refs = refs[:fields], refs[fields:-groups - 1], refs[-groups - 1 :]
    now, sends = refs[0], refs[1:]
    delay = lax.axis_index("delay")
    now[...] = law_of(driving_of(incident, step, terms), sheet, column)
    if step == 2:
        emit(groups, block, sends, 0, now, table)
        return

    @pl.when(delay == 0)
    def _():
        emit(groups, block, sends, 0, now, table)
        if step == 1:
            emit(groups, block, sends, 1, now, other)

    for place, source in enumerate(sources, 1):
        last = place == len(sources)

        @pl.when((delay >= place) if last else (delay == place))
        def _(source=source):
            emit(groups, block, sends, 0, source, table)
            if step == 1:
                emit(groups, block, sends, 1, source, table)


def carry_kernel(section, current, passed, carry):
    delay = lax.axis_index("delay")

    @pl.when(delay == section)
    def _():
        carry[...] = current[...]

    @pl.when(delay != section)
    def _():
        carry[...] = passed[...]


def last_kernel(groups, block, step, sheet, column, incident, matrix, aside, *refs):
    blocks, older, refs = refs[:groups], refs[groups : 2 * groups], refs[2 * groups :]
    terms, now = refs[:-1], refs[-1]
    driving = driving_of(incident, step, terms)
    driving = driving - product(matrix, blocks, 0, block) - product(aside, older, 1, block)
    now[...] = law_of(driving, sheet, column)


def choose_kernel(plan, *refs):
    sources, out = refs[:-1], refs[-1]
    rows = sources[0].shape[0]
    chip = lax.axis_index("delay") // 2
    for z, chosen in enumerate(plan):

        @pl.when(chip == z)
        def _():
            for place, index in enumerate(chosen):
                out[place * rows : (place + 1) * rows, :] = sources[index][...]


def out_kernel(early, early_other, late, late_other, out, sems):
    split = early.shape[0]

    def write(first, second):
        copies = (
            pltpu.make_async_copy(first, out.at[:split], sems.at[0]),
            pltpu.make_async_copy(second, out.at[split:], sems.at[1]),
        )
        for copy in copies:
            copy.start()
        for copy in copies:
            copy.wait()

    odd = lax.axis_index("delay") % 2

    @pl.when(odd == 0)
    def _():
        write(early, late)

    @pl.when(odd == 1)
    def _():
        write(early_other, late_other)


def local(retarded, block_row, block_count, send_pick, history, incident, self_block, sheet_diag):
    groups = lax.axis_size("group")
    delays = lax.axis_size("delay")
    chips = delays // 2
    weights = retarded[0]
    depth, block = weights.shape[1], weights.shape[-1]
    rows, columns = history.shape[1:]
    shape = jax.ShapeDtypeStruct
    piece = lambda parts=1: shape((parts * block, columns), BF16)
    whole = shape((rows, columns), BF16)
    wide_whole = shape((rows, columns), F32)
    bind = functools.partial

    def along(array, pairs):
        return lax.ppermute(array, "delay", pairs)

    def swap(array):
        return along(array, [(d, d ^ 1) for d in range(delays)])

    def shift(array, by=1):
        return along(array, [(d, (d + by) % delays) for d in range(delays)])

    def exchange(sends):
        return [sends[0]] + [
            lax.ppermute(sends[hop], "group", [(g, peer_of(g, hop, groups)) for g in range(groups)])
            for hop in range(1, groups)
        ]

    def gathered(term, first=0):
        other = swap(term)
        chip = call(bind(plus_kernel, first), whole, (), (term, other))
        fields = [chip]
        for z in range(1, chips):
            fields.append(along(chip, [(2 * z, 0)]))
        return fields, other

    earlier = shift(history[0])
    listed = jnp.clip(block_row, 0, rows // block - 1)

    def picked(array):
        return call(bind(pick_kernel, groups, block), [piece()] * groups, (send_pick,), (array,))

    def term_of(blocks, first):
        return call(bind(term_kernel, groups, block, first), whole, (), (dense, *blocks))

    sends = picked(history[0])
    blocks = exchange(sends)
    dense = call(
        bind(dense_kernel, groups, block, depth),
        shape((rows, groups * block), BF16), (listed, block_count), (weights,),
    )
    fields, _ = gathered(term_of(blocks, 0))
    sends = picked(earlier)
    blocks = exchange(sends)
    earlier = shift(earlier)
    inverse = 1.0 / sheet_diag
    column, row = inverse[:, None], inverse[None, :]
    sheet = call(sheet_kernel, shape((rows, rows), BF16), (), (self_block, column, row), 20)
    later, _ = gathered(term_of(blocks, 1))
    other = swap(send_pick)
    oldest = shift(earlier)
    aside = swap(dense)

    law = (sheet, column, incident)
    tables = (send_pick, other)
    found, slots = [], []

    def stepped(step, fields, extra, parts):
        current, *sends = call(
            bind(step_kernel, groups, block, step, len(fields)),
            [whole] + [piece(parts)] * groups, tables, (*law, *fields, *extra),
        )
        found.append(current)
        return sends

    handed = []

    def pass_on():
        handed.append(swap(found[-1]))
        array = handed[-1]
        if slots:
            array = call(bind(carry_kernel, 1), whole, (), (array, slots[-1]))
        slots.append(along(array, [(max(2 * z, 1), 2 * z + 2) for z in range(chips - 1)]))

    def near_of(blocks, first):
        return call(
            bind(near_kernel, groups, block, first), [wide_whole, whole], (), (dense, *blocks)
        )

    sends = stepped(0, fields, (earlier,), 1)
    blocks = exchange(sends)
    pass_on()
    wide, narrow = near_of(blocks, 2)
    fields, _ = gathered(narrow)
    sends = stepped(1, (*later, wide), (handed[0], slots[0], oldest), 2)
    older = exchange(sends)
    pass_on()
    wide, narrow = near_of(older, 1)
    later, partner = gathered(narrow, 2)
    sends = stepped(2, (*fields, wide, partner), (), 1)
    blocks = exchange(sends)
    pass_on()
    found.append(
        call(
            bind(last_kernel, groups, block, 3), whole, (),
            (*law, dense, aside, *blocks, *older, *later),
        )
    )
    carry = call(bind(carry_kernel, 0), whole, (), (found[-1], slots[-1]))
    reach = [STEPS - 1 - step for step in range(STEPS)]
    heads = [z for z in reach if z < chips]
    finals = []
    for k in range(1, chips):
        pairs = [(2 * z, 2 * (z + k)) for z in heads if z + k < chips]
        finals.append(along(found[-1] if len(pairs) == 1 else carry, pairs))

    def origin(step, z):
        beyond = z - reach[step]
        if z == 0:
            return found[step]
        return finals[beyond - 1] if beyond > 0 else slots[step + z - 1]

    def chosen(steps):
        sources, plan = [], []
        for z in range(chips):
            plan.append([])
            for step in steps:
                array = origin(step, z)
                known = [k for k, source in enumerate(sources) if source is array]
                if not known:
                    sources.append(array)
                plan[-1].append(known[0] if known else len(sources) - 1)
        return call(
            bind(choose_kernel, plan), shape((len(steps) * rows, columns), BF16), (), sources
        )

    ready = [s for s in range(STEPS) if chips - 1 <= reach[s]] or [0]
    early = chosen(ready)
    early_other = swap(early)
    late = chosen([s for s in range(STEPS) if s not in ready])
    late_other = swap(late)
    out = pl.pallas_call(
        out_kernel,
        out_shape=shape((STEPS * rows, columns), BF16),
        in_specs=[VMEM] * 4,
        out_specs=pl.BlockSpec(memory_space=pl.ANY),
        scratch_shapes=[pltpu.SemaphoreType.DMA((2,))],
        compiler_params=pltpu.CompilerParams(vmem_limit_bytes=4 << 20),
    )(early, early_other, late, late_other)
    return out.reshape(STEPS, rows, columns)


def solution(mesh):
    placed = (
        P("delay", "group", None, None, None),
        P("delay", "group", None),
        P("delay", "group"),
        P("delay", None, None),
        P("delay", "group", None),
        P(None, "group", None),
        P("group", None),
        P("group"),
    )

    return jax.shard_map(local, mesh=mesh, in_specs=placed, out_specs=P(None, "group", None), check_vma=False)
```

```python
import functools

import jax
import jax.numpy as jnp
from jax import lax
from jax.experimental import pallas as pl
from jax.experimental.pallas import tpu as pltpu
from jax.sharding import PartitionSpec as P


STEPS = 4

F32 = jnp.float32
BF16 = jnp.bfloat16
VMEM = pl.BlockSpec(memory_space=pltpu.VMEM)
SMEM = pl.BlockSpec(memory_space=pltpu.SMEM)


def peer_of(group, hop, groups):
    return group ^ hop if groups & (groups - 1) == 0 else (group + hop) % groups


def source_of(group, hop, groups):
    return group ^ hop if groups & (groups - 1) == 0 else (group - hop) % groups


def call(kernel, out_shape, scalars, arrays, spare=2):
    held = sum(a.size * a.dtype.itemsize for a in (*arrays, *jax.tree.leaves(out_shape)))
    return pl.pallas_call(
        kernel,
        out_shape=out_shape,
        in_specs=[SMEM] * len(scalars) + [VMEM] * len(arrays),
        out_specs=jax.tree.map(lambda _: VMEM, out_shape),
        compiler_params=pltpu.CompilerParams(vmem_limit_bytes=held + spare * (1 << 20)),
    )(*scalars, *arrays)


def dot(a, b):
    return jnp.dot(a, b, preferred_element_type=F32)


def dense_kernel(groups, block, depth, rows, counts, weights, dense):
    me = lax.axis_index("group")
    dense[...] = jnp.zeros_like(dense)
    for hop in range(groups):
        source = source_of(me, hop, groups)
        for entry in range(depth):

            @pl.when(entry < counts[0, source])
            def _():
                start = pl.multiple_of(rows[0, source, entry] * block, block)
                dense[pl.ds(start, block), hop * block : (hop + 1) * block] = weights[source, entry]


def sheet_kernel(self_block, column, row, sheet):
    scaled = self_block[...].astype(F32) * column[...]
    first = scaled.astype(BF16)
    second = dot(first, first)
    total = second - scaled
    third = dot(second.astype(BF16), first)
    sheet[...] = ((total - third) * row[...]).astype(BF16)


def product(matrix, blocks, part, block):
    total = None
    for hop, ref in enumerate(blocks):
        term = dot(matrix[:, hop * block : (hop + 1) * block], ref[part * block : (part + 1) * block, :])
        total = term if total is None else total + term
    return total


def emit(groups, block, sends, part, source, table):
    me = lax.axis_index("group")
    for hop, out in enumerate(sends):
        start = pl.multiple_of(table[0, me, peer_of(me, hop, groups)] * block, block)
        out[part * block : (part + 1) * block, :] = source[pl.ds(start, block), :]


def pick_kernel(groups, block, table, source, *sends):
    emit(groups, block, sends, 0, source, table)


def term_kernel(groups, block, first, matrix, *refs):
    blocks, out = refs[:groups], refs[groups]
    total = product(matrix, blocks, 0, block)
    if first > 0:
        total = jnp.where(lax.axis_index("delay") >= first, total, 0.0)
    out[...] = total.astype(BF16)


def plus_kernel(start, first, second, out):
    total = first[...].astype(F32) + second[...].astype(F32)
    if start > 0:
        total = jnp.where(lax.axis_index("delay") >= start, total, 0.0)
    out[...] = total.astype(BF16)


def near_kernel(groups, block, first, matrix, *refs):
    blocks, wide, narrow = refs[:groups], refs[groups], refs[groups + 1]
    total = product(matrix, blocks, 0, block)
    narrow[...] = jnp.where(lax.axis_index("delay") >= first, total, 0.0).astype(BF16)
    wide[...] = total


def law_of(driving, sheet, column):
    return (driving * column[...] + dot(sheet[...], driving.astype(BF16))).astype(BF16)


def driving_of(incident, step, terms):
    driving = incident[step].astype(F32)
    for ref in terms:
        driving = driving - ref[...].astype(F32)
    return driving


def step_kernel(groups, block, step, fields, table, other, sheet, column, incident, *refs):
    terms, sources, refs = refs[:fields], refs[fields:-groups - 1], refs[-groups - 1 :]
    now, sends = refs[0], refs[1:]
    delay = lax.axis_index("delay")
    now[...] = law_of(driving_of(incident, step, terms), sheet, column)
    if step == 2:
        emit(groups, block, sends, 0, now, table)
        return

    @pl.when(delay == 0)
    def _():
        emit(groups, block, sends, 0, now, table)
        if step == 1:
            emit(groups, block, sends, 1, now, other)

    for place, source in enumerate(sources, 1):
        last = place == len(sources)

        @pl.when((delay >= place) if last else (delay == place))
        def _(source=source):
            emit(groups, block, sends, 0, source, table)
            if step == 1:
                emit(groups, block, sends, 1, source, table)


def carry_kernel(section, current, passed, carry):
    delay = lax.axis_index("delay")

    @pl.when(delay == section)
    def _():
        carry[...] = current[...]

    @pl.when(delay != section)
    def _():
        carry[...] = passed[...]


def last_kernel(groups, block, step, sheet, column, incident, matrix, aside, *refs):
    blocks, older, refs = refs[:groups], refs[groups : 2 * groups], refs[2 * groups :]
    terms, now = refs[:-1], refs[-1]
    driving = driving_of(incident, step, terms)
    driving = driving - product(matrix, blocks, 0, block) - product(aside, older, 1, block)
    now[...] = law_of(driving, sheet, column)


def choose_kernel(plan, *refs):
    sources, out = refs[:-1], refs[-1]
    rows = sources[0].shape[0]
    chip = lax.axis_index("delay") // 2
    for z, chosen in enumerate(plan):

        @pl.when(chip == z)
        def _():
            for place, index in enumerate(chosen):
                out[place * rows : (place + 1) * rows, :] = sources[index][...]


def out_kernel(early, early_other, late, late_other, out, sems):
    split = early.shape[0]

    def write(first, second):
        copies = (
            pltpu.make_async_copy(first, out.at[:split], sems.at[0]),
            pltpu.make_async_copy(second, out.at[split:], sems.at[1]),
        )
        for copy in copies:
            copy.start()
        for copy in copies:
            copy.wait()

    odd = lax.axis_index("delay") % 2

    @pl.when(odd == 0)
    def _():
        write(early, late)

    @pl.when(odd == 1)
    def _():
        write(early_other, late_other)


def local(retarded, block_row, block_count, send_pick, history, incident, self_block, sheet_diag):
    groups = lax.axis_size("group")
    delays = lax.axis_size("delay")
    chips = delays // 2
    weights = retarded[0]
    depth, block = weights.shape[1], weights.shape[-1]
    rows, columns = history.shape[1:]
    shape = jax.ShapeDtypeStruct
    piece = lambda parts=1: shape((parts * block, columns), BF16)
    whole = shape((rows, columns), BF16)
    wide_whole = shape((rows, columns), F32)
    bind = functools.partial

    def along(array, pairs):
        return lax.ppermute(array, "delay", pairs)

    def swap(array):
        return along(array, [(d, d ^ 1) for d in range(delays)])

    def shift(array, by=1):
        return along(array, [(d, (d + by) % delays) for d in range(delays)])

    def exchange(sends):
        return [sends[0]] + [
            lax.ppermute(sends[hop], "group", [(g, peer_of(g, hop, groups)) for g in range(groups)])
            for hop in range(1, groups)
        ]

    def gathered(term, name, first=0):
        other = swap(term)
        chip = call(bind(plus_kernel, first), whole, (), (term, other))
        if name == "3":
            fields = [chip]
            for z in range(1, chips):
                fields.append(along(chip, [(2 * z, 0)]))
            return fields, other
        stride, stage = 1, 1
        while stride < chips:
            if stage > 1:
                chip = call(bind(plus_kernel, 0), whole, (), (chip, came))
            pairs = [(2 * z, 2 * (z - stride)) for z in range(stride, chips, 2 * stride)]
            came = along(chip, pairs)
            stride, stage = 2 * stride, stage + 1
        return [chip, came], other

    earlier = shift(history[0])
    listed = jnp.clip(block_row, 0, rows // block - 1)

    def picked(array):
        return call(bind(pick_kernel, groups, block), [piece()] * groups, (send_pick,), (array,))

    def term_of(blocks, first):
        return call(bind(term_kernel, groups, block, first), whole, (), (dense, *blocks))

    sends = picked(history[0])
    blocks = exchange(sends)
    dense = call(
        bind(dense_kernel, groups, block, depth),
        shape((rows, groups * block), BF16), (listed, block_count), (weights,),
    )
    fields, _ = gathered(term_of(blocks, 0), "0")
    sends = picked(earlier)
    blocks = exchange(sends)
    earlier = shift(earlier)
    inverse = 1.0 / sheet_diag
    column, row = inverse[:, None], inverse[None, :]
    sheet = call(sheet_kernel, shape((rows, rows), BF16), (), (self_block, column, row), 20)
    later, _ = gathered(term_of(blocks, 1), "1")
    other = swap(send_pick)
    oldest = shift(earlier)
    aside = swap(dense)

    law = (sheet, column, incident)
    tables = (send_pick, other)
    found, slots = [], []

    def stepped(step, fields, extra, parts):
        current, *sends = call(
            bind(step_kernel, groups, block, step, len(fields)),
            [whole] + [piece(parts)] * groups, tables, (*law, *fields, *extra),
        )
        found.append(current)
        return sends

    handed = []

    def pass_on():
        handed.append(swap(found[-1]))
        array = handed[-1]
        if slots:
            array = call(bind(carry_kernel, 1), whole, (), (array, slots[-1]))
        slots.append(along(array, [(max(2 * z, 1), 2 * z + 2) for z in range(chips - 1)]))

    def near_of(blocks, first):
        return call(
            bind(near_kernel, groups, block, first), [wide_whole, whole], (), (dense, *blocks)
        )

    sends = stepped(0, fields, (earlier,), 1)
    blocks = exchange(sends)
    pass_on()
    wide, narrow = near_of(blocks, 2)
    fields, _ = gathered(narrow, "2")
    sends = stepped(1, (*later, wide), (handed[0], slots[0], oldest), 2)
    older = exchange(sends)
    pass_on()
    wide, narrow = near_of(older, 1)
    later, partner = gathered(narrow, "3", 2)
    sends = stepped(2, (*fields, wide, partner), (), 1)
    blocks = exchange(sends)
    pass_on()
    found.append(
        call(
            bind(last_kernel, groups, block, 3), whole, (),
            (*law, dense, aside, *blocks, *older, *later),
        )
    )
    carry = call(bind(carry_kernel, 0), whole, (), (found[-1], slots[-1]))
    reach = [STEPS - 1 - step for step in range(STEPS)]
    heads = [z for z in reach if z < chips]
    finals = []
    for k in range(1, chips):
        pairs = [(2 * z, 2 * (z + k)) for z in heads if z + k < chips]
        finals.append(along(found[-1] if len(pairs) == 1 else carry, pairs))

    def origin(step, z):
        beyond = z - reach[step]
        if z == 0:
            return found[step]
        return finals[beyond - 1] if beyond > 0 else slots[step + z - 1]

    def chosen(steps):
        sources, plan = [], []
        for z in range(chips):
            plan.append([])
            for step in steps:
                array = origin(step, z)
                known = [k for k, source in enumerate(sources) if source is array]
                if not known:
                    sources.append(array)
                plan[-1].append(known[0] if known else len(sources) - 1)
        return call(
            bind(choose_kernel, plan), shape((len(steps) * rows, columns), BF16), (), sources
        )

    ready = [s for s in range(STEPS) if chips - 1 <= reach[s]] or [0]
    early = chosen(ready)
    early_other = swap(early)
    late = chosen([s for s in range(STEPS) if s not in ready])
    late_other = swap(late)
    out = pl.pallas_call(
        out_kernel,
        out_shape=shape((STEPS * rows, columns), BF16),
        in_specs=[VMEM] * 4,
        out_specs=pl.BlockSpec(memory_space=pl.ANY),
        scratch_shapes=[pltpu.SemaphoreType.DMA((2,))],
        compiler_params=pltpu.CompilerParams(vmem_limit_bytes=4 << 20),
    )(early, early_other, late, late_other)
    return out.reshape(STEPS, rows, columns)


def solution(mesh):
    placed = (
        P("delay", "group", None, None, None),
        P("delay", "group", None),
        P("delay", "group"),
        P("delay", None, None),
        P("delay", "group", None),
        P(None, "group", None),
        P("group", None),
        P("group"),
    )

    return jax.shard_map(local, mesh=mesh, in_specs=placed, out_specs=P(None, "group", None), check_vma=False)
```

```python
import functools

import jax
import jax.numpy as jnp
from jax import lax
from jax.experimental import pallas as pl
from jax.experimental.pallas import tpu as pltpu
from jax.sharding import PartitionSpec as P


STEPS = 4

F32 = jnp.float32
BF16 = jnp.bfloat16
VMEM = pl.BlockSpec(memory_space=pltpu.VMEM)
SMEM = pl.BlockSpec(memory_space=pltpu.SMEM)


def peer_of(group, hop, groups):
    return group ^ hop if groups & (groups - 1) == 0 else (group + hop) % groups


def source_of(group, hop, groups):
    return group ^ hop if groups & (groups - 1) == 0 else (group - hop) % groups


def call(kernel, out_shape, scalars, arrays, spare=2):
    held = sum(a.size * a.dtype.itemsize for a in (*arrays, *jax.tree.leaves(out_shape)))
    return pl.pallas_call(
        kernel,
        out_shape=out_shape,
        in_specs=[SMEM] * len(scalars) + [VMEM] * len(arrays),
        out_specs=jax.tree.map(lambda _: VMEM, out_shape),
        compiler_params=pltpu.CompilerParams(vmem_limit_bytes=held + spare * (1 << 20)),
    )(*scalars, *arrays)


def dot(a, b):
    return jnp.dot(a, b, preferred_element_type=F32)


def dense_kernel(groups, block, depth, rows, counts, weights, dense):
    me = lax.axis_index("group")
    dense[...] = jnp.zeros_like(dense)
    for hop in range(groups):
        source = source_of(me, hop, groups)
        for entry in range(depth):

            @pl.when(entry < counts[0, source])
            def _():
                start = pl.multiple_of(rows[0, source, entry] * block, block)
                dense[pl.ds(start, block), hop * block : (hop + 1) * block] = weights[source, entry]


def sheet_kernel(self_block, column, row, sheet):
    scaled = self_block[...].astype(F32) * column[...]
    first = scaled.astype(BF16)
    second = dot(first, first)
    total = second - scaled
    third = dot(second.astype(BF16), first)
    sheet[...] = ((total - third) * row[...]).astype(BF16)


def product(matrix, blocks, part, block):
    total = None
    for hop, ref in enumerate(blocks):
        term = dot(matrix[:, hop * block : (hop + 1) * block], ref[part * block : (part + 1) * block, :])
        total = term if total is None else total + term
    return total


def emit(groups, block, sends, part, source, table):
    me = lax.axis_index("group")
    for hop, out in enumerate(sends):
        start = pl.multiple_of(table[0, me, peer_of(me, hop, groups)] * block, block)
        out[part * block : (part + 1) * block, :] = source[pl.ds(start, block), :]


def pick_kernel(groups, block, parts, table, *refs):
    sources, sends = refs[:parts], refs[parts:]
    for part, source in enumerate(sources):
        emit(groups, block, sends, part, source, table)


def term_kernel(groups, block, firsts, matrix, *refs):
    blocks, out = refs[:groups], refs[groups]
    rows = matrix.shape[0]
    for part, first in enumerate(firsts):
        total = product(matrix, blocks, part, block)
        if first > 0:
            total = jnp.where(lax.axis_index("delay") >= first, total, 0.0)
        out[part * rows : (part + 1) * rows, :] = total.astype(BF16)


def plus_kernel(first, second, *outs):
    rows = outs[0].shape[0]
    for part, out in enumerate(outs):
        here = slice(part * rows, (part + 1) * rows)
        out[...] = (first[here, :].astype(F32) + second[here, :].astype(F32)).astype(BF16)


def near_kernel(groups, block, first, matrix, *refs):
    blocks, wide, narrow = refs[:groups], refs[groups], refs[groups + 1]
    total = product(matrix, blocks, 0, block)
    narrow[...] = jnp.where(lax.axis_index("delay") >= first, total, 0.0).astype(BF16)
    wide[...] = total


def law_of(driving, sheet, column):
    return (driving * column[...] + dot(sheet[...], driving.astype(BF16))).astype(BF16)


def driving_of(incident, step, terms):
    driving = incident[step].astype(F32)
    for ref in terms:
        driving = driving - ref[...].astype(F32)
    return driving


def step_kernel(groups, block, step, fields, table, other, sheet, column, incident, *refs):
    terms, sources, refs = refs[:fields], refs[fields:-groups - 1], refs[-groups - 1 :]
    now, sends = refs[0], refs[1:]
    delay = lax.axis_index("delay")
    now[...] = law_of(driving_of(incident, step, terms), sheet, column)
    if step == 2:
        emit(groups, block, sends, 0, now, table)
        return

    @pl.when(delay == 0)
    def _():
        emit(groups, block, sends, 0, now, table)
        if step == 1:
            emit(groups, block, sends, 1, now, other)

    for place, source in enumerate(sources, 1):
        last = place == len(sources)

        @pl.when((delay >= place) if last else (delay == place))
        def _(source=source):
            emit(groups, block, sends, 0, source, table)
            if step == 1:
                emit(groups, block, sends, 1, source, table)


def carry_kernel(section, current, passed, carry):
    delay = lax.axis_index("delay")

    @pl.when(delay == section)
    def _():
        carry[...] = current[...]

    @pl.when(delay != section)
    def _():
        carry[...] = passed[...]


def last_kernel(groups, block, step, sheet, column, incident, matrix, aside, *refs):
    blocks, older, refs = refs[:groups], refs[groups : 2 * groups], refs[2 * groups :]
    terms, now = refs[:-1], refs[-1]
    driving = driving_of(incident, step, terms)
    driving = driving - product(matrix, blocks, 0, block) - product(aside, older, 1, block)
    now[...] = law_of(driving, sheet, column)


def choose_kernel(plan, *refs):
    sources, out = refs[:-1], refs[-1]
    rows = sources[0].shape[0]
    chip = lax.axis_index("delay") // 2
    for z, chosen in enumerate(plan):

        @pl.when(chip == z)
        def _():
            for place, index in enumerate(chosen):
                out[place * rows : (place + 1) * rows, :] = sources[index][...]


def out_kernel(early, early_other, late, late_other, out, sems):
    split = early.shape[0]

    def write(first, second):
        copies = (
            pltpu.make_async_copy(first, out.at[:split], sems.at[0]),
            pltpu.make_async_copy(second, out.at[split:], sems.at[1]),
        )
        for copy in copies:
            copy.start()
        for copy in copies:
            copy.wait()

    odd = lax.axis_index("delay") % 2

    @pl.when(odd == 0)
    def _():
        write(early, late)

    @pl.when(odd == 1)
    def _():
        write(early_other, late_other)


def local(retarded, block_row, block_count, send_pick, history, incident, self_block, sheet_diag):
    groups = lax.axis_size("group")
    delays = lax.axis_size("delay")
    chips = delays // 2
    weights = retarded[0]
    depth, block = weights.shape[1], weights.shape[-1]
    rows, columns = history.shape[1:]
    shape = jax.ShapeDtypeStruct
    piece = lambda parts=1: shape((parts * block, columns), BF16)
    many = lambda count: shape((count * rows, columns), BF16)
    whole, wide_whole = many(1), shape((rows, columns), F32)
    bind = functools.partial

    def along(array, pairs):
        return lax.ppermute(array, "delay", pairs)

    def swap(array):
        return along(array, [(d, d ^ 1) for d in range(delays)])

    def shift(array):
        return along(array, [(d, (d + 1) % delays) for d in range(delays)])

    def exchange(sends):
        return [sends[0]] + [
            lax.ppermute(sends[hop], "group", [(g, peer_of(g, hop, groups)) for g in range(groups)])
            for hop in range(1, groups)
        ]

    def run(kernel, out_shape, scalars, arrays, spare=2):
        return call(kernel, out_shape, scalars, arrays, spare)

    def staged(chip):
        stride, came = 1, None
        while stride < chips:
            if came is not None:
                (chip,) = run(plus_kernel, [whole], (), (chip, came))
            pairs = [(2 * z, 2 * (z - stride)) for z in range(stride, chips, 2 * stride)]
            came = along(chip, pairs)
            stride *= 2
        return [chip, came]

    h1 = shift(history[0])
    listed = jnp.clip(block_row, 0, rows // block - 1)
    pick = lambda arrays: run(
        bind(pick_kernel, groups, block, len(arrays)), [piece(len(arrays))] * groups, (send_pick,), arrays
    )
    term = lambda firsts, blocks: run(bind(term_kernel, groups, block, firsts), many(len(firsts)), (), (dense, *blocks))

    blocks = exchange(pick((history[0],)))
    dense = run(
        bind(dense_kernel, groups, block, depth),
        shape((rows, groups * block), BF16), (listed, block_count), (weights,),
    )
    h2 = shift(h1)
    mine = term((0,), blocks)
    (chip,) = run(plus_kernel, [whole], (), (mine, swap(mine)))
    field0 = staged(chip)
    blocks = exchange(pick((h1, h2)))
    h3 = shift(h2)
    inverse = 1.0 / sheet_diag
    column, row = inverse[:, None], inverse[None, :]
    sheet = run(sheet_kernel, shape((rows, rows), BF16), (), (self_block, column, row), 20)
    mine = term((1, 2), blocks)
    chip1, chip2 = run(plus_kernel, [whole, whole], (), (mine, swap(mine)))
    field1, field2 = staged(chip1), staged(chip2)
    other = swap(send_pick)
    aside = swap(dense)

    law = (sheet, column, incident)
    found, slots = [], []

    def stepped(step, fields, extra, parts):
        current, *sends = run(
            bind(step_kernel, groups, block, step, len(fields)),
            [whole] + [piece(parts)] * groups, (send_pick, other), (*law, *fields, *extra),
        )
        found.append(current)
        return sends

    def pass_on():
        handed = array = swap(found[-1])
        if slots:
            array = run(bind(carry_kernel, 1), whole, (), (array, slots[-1]))
        pairs = [(max(2 * z, 1), 2 * z + 2) for z in range(chips - 1)]
        slots.append(along(array, pairs))
        return handed

    def near_of(blocks, first):
        return run(bind(near_kernel, groups, block, first), [wide_whole, whole], (), (dense, *blocks))

    blocks = exchange(stepped(0, field0, (h3,), 1))
    handed = pass_on()
    wide, narrow = near_of(blocks, 3)
    (chip,) = run(plus_kernel, [whole], (), (narrow, swap(narrow)))
    field3 = staged(chip)
    older = exchange(stepped(1, (*field1, wide), (handed, slots[0]), 2))
    pass_on()
    wide, narrow = near_of(older, 1)
    partner = swap(narrow)
    second = along(narrow, [(2, 0)])
    blocks = exchange(stepped(2, (*field2, wide, partner), (), 1))
    pass_on()
    found.append(
        run(
            bind(last_kernel, groups, block, 3), whole, (),
            (*law, dense, aside, *blocks, *older, *field3, second),
        )
    )
    carry = run(bind(carry_kernel, 0), whole, (), (found[-1], slots[-1]))
    reach = [STEPS - 1 - step for step in range(STEPS)]
    heads = [z for z in reach if z < chips]
    finals = []
    for k in range(1, chips):
        pairs = [(2 * z, 2 * (z + k)) for z in heads if z + k < chips]
        finals.append(along(found[-1] if len(pairs) == 1 else carry, pairs))

    def origin(step, z):
        beyond = z - reach[step]
        if z == 0:
            return found[step]
        return finals[beyond - 1] if beyond > 0 else slots[step + z - 1]

    def chosen(steps):
        sources, plan = [], []
        for z in range(chips):
            plan.append([])
            for step in steps:
                array = origin(step, z)
                known = [k for k, source in enumerate(sources) if source is array]
                if not known:
                    sources.append(array)
                plan[-1].append(known[0] if known else len(sources) - 1)
        return run(bind(choose_kernel, plan), many(len(steps)), (), sources)

    ready = [s for s in range(STEPS) if chips - 1 <= reach[s]] or [0]
    early = chosen(ready)
    early_other = swap(early)
    late = chosen([s for s in range(STEPS) if s not in ready])
    late_other = swap(late)
    out = pl.pallas_call(
        out_kernel,
        out_shape=many(STEPS),
        in_specs=[VMEM] * 4,
        out_specs=pl.BlockSpec(memory_space=pl.ANY),
        scratch_shapes=[pltpu.SemaphoreType.DMA((2,))],
        compiler_params=pltpu.CompilerParams(vmem_limit_bytes=4 << 20),
    )(early, early_other, late, late_other)
    return out.reshape(STEPS, rows, columns)


def solution(mesh):
    placed = (
        P("delay", "group", None, None, None),
        P("delay", "group", None),
        P("delay", "group"),
        P("delay", None, None),
        P("delay", "group", None),
        P(None, "group", None),
        P("group", None),
        P("group"),
    )

    return jax.shard_map(local, mesh=mesh, in_specs=placed, out_specs=P(None, "group", None), check_vma=False)
```

```python
import functools

import jax
import jax.numpy as jnp
from jax import lax
from jax.experimental import pallas as pl
from jax.experimental.pallas import tpu as pltpu
from jax.sharding import PartitionSpec as P


STEPS = 4

F32 = jnp.float32
BF16 = jnp.bfloat16
VMEM = pl.BlockSpec(memory_space=pltpu.VMEM)
SMEM = pl.BlockSpec(memory_space=pltpu.SMEM)


def peer_of(group, hop, groups):
    return group ^ hop if groups & (groups - 1) == 0 else (group + hop) % groups


def source_of(group, hop, groups):
    return group ^ hop if groups & (groups - 1) == 0 else (group - hop) % groups


def call(kernel, out_shape, scalars, arrays, spare=2):
    held = sum(a.size * a.dtype.itemsize for a in (*arrays, *jax.tree.leaves(out_shape)))
    return pl.pallas_call(
        kernel,
        out_shape=out_shape,
        in_specs=[SMEM] * len(scalars) + [VMEM] * len(arrays),
        out_specs=jax.tree.map(lambda _: VMEM, out_shape),
        compiler_params=pltpu.CompilerParams(vmem_limit_bytes=held + spare * (1 << 20)),
    )(*scalars, *arrays)


def dot(a, b):
    return jnp.dot(a, b, preferred_element_type=F32)


def dense_kernel(groups, block, depth, rows, counts, weights, dense):
    me = lax.axis_index("group")
    dense[...] = jnp.zeros_like(dense)
    for hop in range(groups):
        source = source_of(me, hop, groups)
        for entry in range(depth):

            @pl.when(entry < counts[0, source])
            def _():
                start = pl.multiple_of(rows[0, source, entry] * block, block)
                dense[pl.ds(start, block), hop * block : (hop + 1) * block] = weights[source, entry]


def sheet_kernel(self_block, column, row, sheet):
    scaled = self_block[...].astype(F32) * column[...]
    first = scaled.astype(BF16)
    second = dot(first, first)
    total = second - scaled
    third = dot(second.astype(BF16), first)
    sheet[...] = ((total - third) * row[...]).astype(BF16)


def product(matrix, blocks, part, block):
    total = None
    for hop, ref in enumerate(blocks):
        term = dot(matrix[:, hop * block : (hop + 1) * block], ref[part * block : (part + 1) * block, :])
        total = term if total is None else total + term
    return total


def emit(groups, block, sends, part, source, table):
    me = lax.axis_index("group")
    for hop, out in enumerate(sends):
        start = pl.multiple_of(table[0, me, peer_of(me, hop, groups)] * block, block)
        out[part * block : (part + 1) * block, :] = source[pl.ds(start, block), :]


def pick_kernel(groups, block, parts, table, *refs):
    sources, sends = refs[:parts], refs[parts:]
    for part, source in enumerate(sources):
        emit(groups, block, sends, part, source, table)


def term_kernel(groups, block, firsts, matrix, *refs):
    blocks, out = refs[:groups], refs[groups]
    rows = matrix.shape[0]
    for part, first in enumerate(firsts):
        total = product(matrix, blocks, part, block)
        if first > 0:
            total = jnp.where(lax.axis_index("delay") >= first, total, 0.0)
        out[part * rows : (part + 1) * rows, :] = total.astype(BF16)


def plus_kernel(first, second, *outs):
    rows = outs[0].shape[0]
    for part, out in enumerate(outs):
        here = slice(part * rows, (part + 1) * rows)
        out[...] = (first[here, :].astype(F32) + second[here, :].astype(F32)).astype(BF16)


def near_kernel(groups, block, first, matrix, *refs):
    blocks, wide, narrow = refs[:groups], refs[groups], refs[groups + 1]
    total = product(matrix, blocks, 0, block)
    narrow[...] = jnp.where(lax.axis_index("delay") >= first, total, 0.0).astype(BF16)
    wide[...] = total


def law_of(driving, sheet, column):
    return (driving * column[...] + dot(sheet[...], driving.astype(BF16))).astype(BF16)


def driving_of(incident, step, terms):
    driving = incident[step].astype(F32)
    for ref in terms:
        driving = driving - ref[...].astype(F32)
    return driving


def step_kernel(groups, block, step, fields, table, other, sheet, column, incident, *refs):
    terms, sources, refs = refs[:fields], refs[fields:-groups - 1], refs[-groups - 1 :]
    now, sends = refs[0], refs[1:]
    delay = lax.axis_index("delay")
    now[...] = law_of(driving_of(incident, step, terms), sheet, column)
    if step == 2:
        emit(groups, block, sends, 0, now, table)
        return

    @pl.when(delay == 0)
    def _():
        emit(groups, block, sends, 0, now, table)
        if step == 1:
            emit(groups, block, sends, 1, now, other)

    for place, source in enumerate(sources, 1):
        last = place == len(sources)

        @pl.when((delay >= place) if last else (delay == place))
        def _(source=source):
            emit(groups, block, sends, 0, source, table)
            if step == 1:
                emit(groups, block, sends, 1, source, table)


def carry_kernel(section, current, passed, carry):
    delay = lax.axis_index("delay")

    @pl.when(delay == section)
    def _():
        carry[...] = current[...]

    @pl.when(delay != section)
    def _():
        carry[...] = passed[...]


def last_kernel(groups, block, step, sheet, column, incident, matrix, aside, *refs):
    blocks, older, refs = refs[:groups], refs[groups : 2 * groups], refs[2 * groups :]
    terms, now = refs[:-1], refs[-1]
    driving = driving_of(incident, step, terms)
    driving = driving - product(matrix, blocks, 0, block) - product(aside, older, 1, block)
    now[...] = law_of(driving, sheet, column)


def choose_kernel(plan, *refs):
    sources, out = refs[:-1], refs[-1]
    rows = sources[0].shape[0]
    chip = lax.axis_index("delay") // 2
    for z, chosen in enumerate(plan):

        @pl.when(chip == z)
        def _():
            for place, index in enumerate(chosen):
                out[place * rows : (place + 1) * rows, :] = sources[index][...]


def out_kernel(early, early_other, late, late_other, out, sems):
    split = early.shape[0]

    def write(first, second):
        copies = (
            pltpu.make_async_copy(first, out.at[:split], sems.at[0]),
            pltpu.make_async_copy(second, out.at[split:], sems.at[1]),
        )
        for copy in copies:
            copy.start()
        for copy in copies:
            copy.wait()

    odd = lax.axis_index("delay") % 2

    @pl.when(odd == 0)
    def _():
        write(early, late)

    @pl.when(odd == 1)
    def _():
        write(early_other, late_other)


def local(retarded, block_row, block_count, send_pick, history, incident, self_block, sheet_diag):
    groups = lax.axis_size("group")
    delays = lax.axis_size("delay")
    chips = delays // 2
    weights = retarded[0]
    depth, block = weights.shape[1], weights.shape[-1]
    rows, columns = history.shape[1:]
    shape = jax.ShapeDtypeStruct
    piece = lambda parts=1: shape((parts * block, columns), BF16)
    many = lambda count: shape((count * rows, columns), BF16)
    whole, wide_whole = many(1), shape((rows, columns), F32)
    bind = functools.partial

    def along(array, pairs):
        return lax.ppermute(array, "delay", pairs)

    def swap(array):
        return along(array, [(d, d ^ 1) for d in range(delays)])

    def shift(array):
        return along(array, [(d, (d + 1) % delays) for d in range(delays)])

    def exchange(sends):
        return [sends[0]] + [
            lax.ppermute(sends[hop], "group", [(g, peer_of(g, hop, groups)) for g in range(groups)])
            for hop in range(1, groups)
        ]

    def run(kernel, out_shape, scalars, arrays, spare=2):
        return call(kernel, out_shape, scalars, arrays, spare)

    def staged(chip):
        stride, came = 1, None
        while stride < chips:
            if came is not None:
                (chip,) = run(plus_kernel, [whole], (), (chip, came))
            pairs = [(2 * z, 2 * (z - stride)) for z in range(stride, chips, 2 * stride)]
            came = along(chip, pairs)
            stride *= 2
        return [chip, came]

    def direct(chip):
        return [chip] + [along(chip, [(2 * z, 0)]) for z in range(1, chips)]

    h1 = shift(history[0])
    listed = jnp.clip(block_row, 0, rows // block - 1)
    pick = lambda arrays: run(
        bind(pick_kernel, groups, block, len(arrays)), [piece(len(arrays))] * groups, (send_pick,), arrays
    )
    term = lambda firsts, blocks: run(bind(term_kernel, groups, block, firsts), many(len(firsts)), (), (dense, *blocks))

    blocks = exchange(pick((history[0],)))
    dense = run(
        bind(dense_kernel, groups, block, depth),
        shape((rows, groups * block), BF16), (listed, block_count), (weights,),
    )
    h2 = shift(h1)
    mine = term((0,), blocks)
    (chip,) = run(plus_kernel, [whole], (), (mine, swap(mine)))
    field0 = staged(chip)
    blocks = exchange(pick((h1, h2)))
    h3 = shift(h2)
    inverse = 1.0 / sheet_diag
    column, row = inverse[:, None], inverse[None, :]
    sheet = run(sheet_kernel, shape((rows, rows), BF16), (), (self_block, column, row), 20)
    mine = term((1, 2), blocks)
    chip1, chip2 = run(plus_kernel, [whole, whole], (), (mine, swap(mine)))
    field1, field2 = direct(chip1), staged(chip2)
    other = swap(send_pick)
    aside = swap(dense)

    law = (sheet, column, incident)
    found, slots = [], []

    def stepped(step, fields, extra, parts):
        current, *sends = run(
            bind(step_kernel, groups, block, step, len(fields)),
            [whole] + [piece(parts)] * groups, (send_pick, other), (*law, *fields, *extra),
        )
        found.append(current)
        return sends

    def pass_on(core=1):
        handed = array = swap(found[-1]) if core else found[-1]
        if slots:
            array = run(bind(carry_kernel, core), whole, (), (array, slots[-1]))
        pairs = [(max(2 * z, core), 2 * z + 2) for z in range(chips - 1)]
        slots.append(along(array, pairs))
        return handed

    def near_of(blocks, first):
        return run(bind(near_kernel, groups, block, first), [wide_whole, whole], (), (dense, *blocks))

    blocks = exchange(stepped(0, field0, (h3,), 1))
    handed = pass_on()
    wide, narrow = near_of(blocks, 3)
    (chip,) = run(plus_kernel, [whole], (), (narrow, swap(narrow)))
    field3 = staged(chip)
    older = exchange(stepped(1, (*field1, wide), (handed, slots[0]), 2))
    pass_on()
    wide, narrow = near_of(older, 1)
    partner = swap(narrow)
    second = along(narrow, [(2, 0)])
    blocks = exchange(stepped(2, (*field2, wide, partner), (), 1))
    pass_on(0)
    found.append(
        run(
            bind(last_kernel, groups, block, 3), whole, (),
            (*law, dense, aside, *blocks, *older, *field3, second),
        )
    )
    carry = run(bind(carry_kernel, 0), whole, (), (found[-1], slots[-1]))
    reach = [STEPS - 1 - step for step in range(STEPS)]
    heads = [z for z in reach if z < chips]
    finals = []
    for k in range(1, chips):
        pairs = [(2 * z, 2 * (z + k)) for z in heads if z + k < chips]
        finals.append(along(found[-1] if len(pairs) == 1 else carry, pairs))

    def origin(step, z):
        beyond = z - reach[step]
        if z == 0:
            return found[step]
        return finals[beyond - 1] if beyond > 0 else slots[step + z - 1]

    def chosen(steps):
        sources, plan = [], []
        for z in range(chips):
            plan.append([])
            for step in steps:
                array = origin(step, z)
                known = [k for k, source in enumerate(sources) if source is array]
                if not known:
                    sources.append(array)
                plan[-1].append(known[0] if known else len(sources) - 1)
        return run(bind(choose_kernel, plan), many(len(steps)), (), sources)

    ready = [s for s in range(STEPS) if chips - 1 <= reach[s]] or [0]
    early = chosen(ready)
    early_other = swap(early)
    late = chosen([s for s in range(STEPS) if s not in ready])
    late_other = swap(late)
    out = pl.pallas_call(
        out_kernel,
        out_shape=many(STEPS),
        in_specs=[VMEM] * 4,
        out_specs=pl.BlockSpec(memory_space=pl.ANY),
        scratch_shapes=[pltpu.SemaphoreType.DMA((2,))],
        compiler_params=pltpu.CompilerParams(vmem_limit_bytes=4 << 20),
    )(early, early_other, late, late_other)
    return out.reshape(STEPS, rows, columns)


def solution(mesh):
    placed = (
        P("delay", "group", None, None, None),
        P("delay", "group", None),
        P("delay", "group"),
        P("delay", None, None),
        P("delay", "group", None),
        P(None, "group", None),
        P("group", None),
        P("group"),
    )

    return jax.shard_map(local, mesh=mesh, in_specs=placed, out_specs=P(None, "group", None), check_vma=False)
```

```python
import functools

import jax
import jax.numpy as jnp
from jax import lax
from jax.experimental import pallas as pl
from jax.experimental.pallas import tpu as pltpu
from jax.sharding import PartitionSpec as P


STEPS = 4

F32 = jnp.float32
BF16 = jnp.bfloat16
VMEM = pl.BlockSpec(memory_space=pltpu.VMEM)
SMEM = pl.BlockSpec(memory_space=pltpu.SMEM)


def peer_of(group, hop, groups):
    return group ^ hop if groups & (groups - 1) == 0 else (group + hop) % groups


def source_of(group, hop, groups):
    return group ^ hop if groups & (groups - 1) == 0 else (group - hop) % groups


def call(kernel, out_shape, scalars, arrays, spare=2):
    held = sum(a.size * a.dtype.itemsize for a in (*arrays, *jax.tree.leaves(out_shape)))
    return pl.pallas_call(
        kernel,
        out_shape=out_shape,
        in_specs=[SMEM] * len(scalars) + [VMEM] * len(arrays),
        out_specs=jax.tree.map(lambda _: VMEM, out_shape),
        compiler_params=pltpu.CompilerParams(vmem_limit_bytes=held + spare * (1 << 20)),
    )(*scalars, *arrays)


def dot(a, b):
    return jnp.dot(a, b, preferred_element_type=F32)


def dense_kernel(groups, block, depth, rows, counts, weights, dense):
    me = lax.axis_index("group")
    dense[...] = jnp.zeros_like(dense)
    for hop in range(groups):
        source = source_of(me, hop, groups)
        for entry in range(depth):

            @pl.when(entry < counts[0, source])
            def _():
                start = pl.multiple_of(rows[0, source, entry] * block, block)
                dense[pl.ds(start, block), hop * block : (hop + 1) * block] = weights[source, entry]


def sheet_kernel(self_block, column, row, sheet):
    scaled = self_block[...].astype(F32) * column[...]
    first = scaled.astype(BF16)
    second = dot(first, first)
    total = second - scaled
    third = dot(second.astype(BF16), first)
    sheet[...] = ((total - third) * row[...]).astype(BF16)


def product(matrix, blocks, part, block):
    total = None
    for hop, ref in enumerate(blocks):
        term = dot(matrix[:, hop * block : (hop + 1) * block], ref[part * block : (part + 1) * block, :])
        total = term if total is None else total + term
    return total


def emit(groups, block, sends, part, source, table):
    me = lax.axis_index("group")
    for hop, out in enumerate(sends):
        start = pl.multiple_of(table[0, me, peer_of(me, hop, groups)] * block, block)
        out[part * block : (part + 1) * block, :] = source[pl.ds(start, block), :]


def pick_kernel(groups, block, parts, table, *refs):
    sources, sends = refs[:parts], refs[parts:]
    for part, source in enumerate(sources):
        emit(groups, block, sends, part, source, table)


def term_kernel(groups, block, firsts, matrix, *refs):
    blocks, out = refs[:groups], refs[groups]
    rows = matrix.shape[0]
    for part, first in enumerate(firsts):
        total = product(matrix, blocks, part, block)
        if first > 0:
            total = jnp.where(lax.axis_index("delay") >= first, total, 0.0)
        out[part * rows : (part + 1) * rows, :] = total.astype(BF16)


def plus_kernel(first, second, *outs):
    rows = outs[0].shape[0]
    for part, out in enumerate(outs):
        here = slice(part * rows, (part + 1) * rows)
        out[...] = (first[here, :].astype(F32) + second[here, :].astype(F32)).astype(BF16)


def near_kernel(groups, block, first, matrix, *refs):
    blocks, wide, narrow = refs[:groups], refs[groups], refs[groups + 1]
    total = product(matrix, blocks, 0, block)
    narrow[...] = jnp.where(lax.axis_index("delay") >= first, total, 0.0).astype(BF16)
    wide[...] = total


def law_of(driving, sheet, column):
    return (driving * column[...] + dot(sheet[...], driving.astype(BF16))).astype(BF16)


def driving_of(incident, step, terms):
    driving = incident[step].astype(F32)
    for ref in terms:
        driving = driving - ref[...].astype(F32)
    return driving


def step_kernel(groups, block, step, fields, table, other, sheet, column, incident, *refs):
    terms, sources, refs = refs[:fields], refs[fields:-groups - 1], refs[-groups - 1 :]
    now, sends = refs[0], refs[1:]
    delay = lax.axis_index("delay")
    now[...] = law_of(driving_of(incident, step, terms), sheet, column)
    if step == 2:
        emit(groups, block, sends, 0, now, table)
        return

    @pl.when(delay == 0)
    def _():
        emit(groups, block, sends, 0, now, table)
        if step == 1:
            emit(groups, block, sends, 1, now, other)

    for place, source in enumerate(sources, 1):
        last = place == len(sources)

        @pl.when((delay >= place) if last else (delay == place))
        def _(source=source):
            emit(groups, block, sends, 0, source, table)
            if step == 1:
                emit(groups, block, sends, 1, source, table)


def carry_kernel(section, current, passed, carry):
    delay = lax.axis_index("delay")

    @pl.when(delay == section)
    def _():
        carry[...] = current[...]

    @pl.when(delay != section)
    def _():
        carry[...] = passed[...]


def last_kernel(groups, block, step, sheet, column, incident, matrix, aside, *refs):
    blocks, older, refs = refs[:groups], refs[groups : 2 * groups], refs[2 * groups :]
    terms, now = refs[:-1], refs[-1]
    driving = driving_of(incident, step, terms)
    driving = driving - product(matrix, blocks, 0, block) - product(aside, older, 1, block)
    now[...] = law_of(driving, sheet, column)


def choose_kernel(plan, *refs):
    sources, out = refs[:-1], refs[-1]
    rows = sources[0].shape[0]
    chip = lax.axis_index("delay") // 2
    for z, chosen in enumerate(plan):

        @pl.when(chip == z)
        def _():
            for place, index in enumerate(chosen):
                out[place * rows : (place + 1) * rows, :] = sources[index][...]


def out_kernel(early, early_other, late, late_other, out, sems):
    split = early.shape[0]

    def write(first, second):
        copies = (
            pltpu.make_async_copy(first, out.at[:split], sems.at[0]),
            pltpu.make_async_copy(second, out.at[split:], sems.at[1]),
        )
        for copy in copies:
            copy.start()
        for copy in copies:
            copy.wait()

    odd = lax.axis_index("delay") % 2

    @pl.when(odd == 0)
    def _():
        write(early, late)

    @pl.when(odd == 1)
    def _():
        write(early_other, late_other)


def local(retarded, block_row, block_count, send_pick, history, incident, self_block, sheet_diag):
    groups = lax.axis_size("group")
    delays = lax.axis_size("delay")
    chips = delays // 2
    weights = retarded[0]
    depth, block = weights.shape[1], weights.shape[-1]
    rows, columns = history.shape[1:]
    shape = jax.ShapeDtypeStruct
    piece = lambda parts=1: shape((parts * block, columns), BF16)
    many = lambda count: shape((count * rows, columns), BF16)
    whole, wide_whole = many(1), shape((rows, columns), F32)
    bind = functools.partial

    def along(array, pairs):
        return lax.ppermute(array, "delay", pairs)

    def swap(array):
        return along(array, [(d, d ^ 1) for d in range(delays)])

    def shift(array):
        return along(array, [(d, (d + 1) % delays) for d in range(delays)])

    def exchange(sends):
        got = [sends[0]]
        for hop in range(1, groups):
            pairs = [(g, peer_of(g, hop, groups)) for g in range(groups)]
            got.append(lax.ppermute(sends[hop], "group", pairs))
        return got

    def run(kernel, out_shape, scalars, arrays, spare=2):
        return call(kernel, out_shape, scalars, arrays, spare)

    def staged(chip):
        stride, came = 1, None
        while stride < chips:
            if came is not None:
                (chip,) = run(plus_kernel, [whole], (), (chip, came))
            pairs = [(2 * z, 2 * (z - stride)) for z in range(stride, chips, 2 * stride)]
            came = along(chip, pairs)
            stride *= 2
        return [chip, came]

    def direct(chip):
        return [chip] + [along(chip, [(2 * z, 0)]) for z in range(1, chips)]

    h1 = shift(history[0])
    listed = jnp.clip(block_row, 0, rows // block - 1)
    pick = lambda arrays: run(
        bind(pick_kernel, groups, block, len(arrays)), [piece(len(arrays))] * groups, (send_pick,), arrays
    )
    term = lambda firsts, blocks: run(bind(term_kernel, groups, block, firsts), many(len(firsts)), (), (dense, *blocks))

    blocks = exchange(pick((history[0],)))
    dense = run(
        bind(dense_kernel, groups, block, depth),
        shape((rows, groups * block), BF16), (listed, block_count), (weights,),
    )
    h2 = shift(h1)
    mine = term((0,), blocks)
    (chip,) = run(plus_kernel, [whole], (), (mine, swap(mine)))
    field0 = staged(chip)
    blocks = exchange(pick((h1, h2)))
    h3 = shift(h2)
    inverse = 1.0 / sheet_diag
    column, row = inverse[:, None], inverse[None, :]
    sheet = run(sheet_kernel, shape((rows, rows), BF16), (), (self_block, column, row), 20)
    mine = term((1, 2), blocks)
    chip1, chip2 = run(plus_kernel, [whole, whole], (), (mine, swap(mine)))
    field1, field2 = direct(chip1), staged(chip2)
    other = swap(send_pick)
    aside = swap(dense)

    law = (sheet, column, incident)
    found, slots = [], []

    def stepped(step, fields, extra, parts):
        current, *sends = run(
            bind(step_kernel, groups, block, step, len(fields)),
            [whole] + [piece(parts)] * groups, (send_pick, other), (*law, *fields, *extra),
        )
        found.append(current)
        return sends

    def pass_on(core=1):
        handed = array = swap(found[-1]) if core else found[-1]
        if slots:
            array = run(bind(carry_kernel, core), whole, (), (array, slots[-1]))
        pairs = [(max(2 * z, core), 2 * z + 2) for z in range(chips - 1)]
        slots.append(along(array, pairs))
        return handed

    def near_of(blocks, first):
        return run(bind(near_kernel, groups, block, first), [wide_whole, whole], (), (dense, *blocks))

    blocks = exchange(stepped(0, field0, (h3,), 1))
    handed = pass_on()
    wide, narrow = near_of(blocks, 3)
    (chip,) = run(plus_kernel, [whole], (), (narrow, swap(narrow)))
    field3 = staged(chip)
    older = exchange(stepped(1, (*field1, wide), (handed, slots[0]), 2))
    pass_on()
    wide, narrow = near_of(older, 1)
    partner = swap(narrow)
    second = along(narrow, [(2, 0)])
    blocks = exchange(stepped(2, (*field2, wide, partner), (), 1))
    pass_on(0)
    found.append(
        run(
            bind(last_kernel, groups, block, 3), whole, (),
            (*law, dense, aside, *blocks, *older, *field3, second),
        )
    )
    carry = run(bind(carry_kernel, 0), whole, (), (found[-1], slots[-1]))
    reach = [STEPS - 1 - step for step in range(STEPS)]
    heads = [z for z in reach if z < chips]
    finals = []
    for k in range(1, chips):
        pairs = [(2 * z, 2 * (z + k)) for z in heads if z + k < chips]
        finals.append(along(found[-1] if len(pairs) == 1 else carry, pairs))

    def origin(step, z):
        beyond = z - reach[step]
        if z == 0:
            return found[step]
        return finals[beyond - 1] if beyond > 0 else slots[step + z - 1]

    def chosen(steps):
        sources, plan = [], []
        for z in range(chips):
            plan.append([])
            for step in steps:
                array = origin(step, z)
                known = [k for k, source in enumerate(sources) if source is array]
                if not known:
                    sources.append(array)
                plan[-1].append(known[0] if known else len(sources) - 1)
        return run(bind(choose_kernel, plan), many(len(steps)), (), sources)

    ready = [s for s in range(STEPS) if chips - 1 <= reach[s]] or [0]
    early = chosen(ready)
    early_other = swap(early)
    late = chosen([s for s in range(STEPS) if s not in ready])
    late_other = swap(late)
    out = pl.pallas_call(
        out_kernel,
        out_shape=many(STEPS),
        in_specs=[VMEM] * 4,
        out_specs=pl.BlockSpec(memory_space=pl.ANY),
        scratch_shapes=[pltpu.SemaphoreType.DMA((2,))],
        compiler_params=pltpu.CompilerParams(vmem_limit_bytes=4 << 20),
    )(early, early_other, late, late_other)
    return out.reshape(STEPS, rows, columns)


def solution(mesh):
    placed = (
        P("delay", "group", None, None, None),
        P("delay", "group", None),
        P("delay", "group"),
        P("delay", None, None),
        P("delay", "group", None),
        P(None, "group", None),
        P("group", None),
        P("group"),
    )

    return jax.shard_map(local, mesh=mesh, in_specs=placed, out_specs=P(None, "group", None), check_vma=False)
```

```python
import functools

import jax
import jax.numpy as jnp
from jax import lax
from jax.experimental import pallas as pl
from jax.experimental.pallas import tpu as pltpu
from jax.sharding import PartitionSpec as P


STEPS = 4

F32 = jnp.float32
BF16 = jnp.bfloat16
VMEM = pl.BlockSpec(memory_space=pltpu.VMEM)
SMEM = pl.BlockSpec(memory_space=pltpu.SMEM)


def peer_of(group, hop, groups):
    return group ^ hop if groups & (groups - 1) == 0 else (group + hop) % groups


def source_of(group, hop, groups):
    return group ^ hop if groups & (groups - 1) == 0 else (group - hop) % groups


def call(kernel, out_shape, scalars, arrays, spare=2):
    held = sum(a.size * a.dtype.itemsize for a in (*arrays, *jax.tree.leaves(out_shape)))
    return pl.pallas_call(
        kernel,
        out_shape=out_shape,
        in_specs=[SMEM] * len(scalars) + [VMEM] * len(arrays),
        out_specs=jax.tree.map(lambda _: VMEM, out_shape),
        compiler_params=pltpu.CompilerParams(vmem_limit_bytes=held + spare * (1 << 20)),
    )(*scalars, *arrays)


def dot(a, b):
    return jnp.dot(a, b, preferred_element_type=F32)


def dense_kernel(groups, block, depth, rows, counts, weights, dense):
    me = lax.axis_index("group")
    dense[...] = jnp.zeros_like(dense)
    for hop in range(groups):
        source = source_of(me, hop, groups)
        for entry in range(depth):

            @pl.when(entry < counts[0, source])
            def _():
                start = pl.multiple_of(rows[0, source, entry] * block, block)
                dense[pl.ds(start, block), hop * block : (hop + 1) * block] = weights[source, entry]


def sheet_kernel(self_block, diagonal, sheet, column):
    row = 1.0 / diagonal[...]
    column[...] = jnp.broadcast_to(row, (column.shape[1], row.shape[1])).T
    scaled = self_block[...].astype(F32) * column[:, :1]
    first = scaled.astype(BF16)
    second = dot(first, first)
    total = second - scaled
    third = dot(second.astype(BF16), first)
    sheet[...] = ((total - third) * row).astype(BF16)


def product(matrix, blocks, part, block):
    total = None
    for hop, ref in enumerate(blocks):
        term = dot(matrix[:, hop * block : (hop + 1) * block], ref[part * block : (part + 1) * block, :])
        total = term if total is None else total + term
    return total


def emit(groups, block, sends, part, source, table):
    me = lax.axis_index("group")
    for hop, out in enumerate(sends):
        start = pl.multiple_of(table[0, me, peer_of(me, hop, groups)] * block, block)
        out[part * block : (part + 1) * block, :] = source[pl.ds(start, block), :]


def pick_kernel(groups, block, parts, table, *refs):
    sources, sends = refs[:parts], refs[parts:]
    for part, source in enumerate(sources):
        emit(groups, block, sends, part, source, table)


def term_kernel(groups, block, firsts, matrix, *refs):
    blocks, out = refs[:groups], refs[groups]
    rows = matrix.shape[0]
    for part, first in enumerate(firsts):
        total = product(matrix, blocks, part, block)
        if first > 0:
            total = jnp.where(lax.axis_index("delay") >= first, total, 0.0)
        out[part * rows : (part + 1) * rows, :] = total.astype(BF16)


def plus_kernel(first, second, *outs):
    rows = outs[0].shape[0]
    for part, out in enumerate(outs):
        here = slice(part * rows, (part + 1) * rows)
        out[...] = (first[here, :].astype(F32) + second[here, :].astype(F32)).astype(BF16)


def near_kernel(groups, block, first, matrix, *refs):
    blocks, wide, narrow = refs[:groups], refs[groups], refs[groups + 1]
    total = product(matrix, blocks, 0, block)
    narrow[...] = jnp.where(lax.axis_index("delay") >= first, total, 0.0).astype(BF16)
    wide[...] = total


def law_of(driving, sheet, column):
    return (driving * column[...] + dot(sheet[...], driving.astype(BF16))).astype(BF16)


def driving_of(incident, step, terms):
    driving = incident[step].astype(F32)
    for ref in terms:
        driving = driving - ref[...].astype(F32)
    return driving


def step_kernel(groups, block, step, fields, table, other, sheet, column, incident, *refs):
    terms, sources, refs = refs[:fields], refs[fields:-groups - 1], refs[-groups - 1 :]
    now, sends = refs[0], refs[1:]
    delay = lax.axis_index("delay")
    now[...] = law_of(driving_of(incident, step, terms), sheet, column)
    if step == 2:
        emit(groups, block, sends, 0, now, table)
        return

    @pl.when(delay == 0)
    def _():
        emit(groups, block, sends, 0, now, table)
        if step == 1:
            emit(groups, block, sends, 1, now, other)

    for place, source in enumerate(sources, 1):
        last = place == len(sources)

        @pl.when((delay >= place) if last else (delay == place))
        def _(source=source):
            emit(groups, block, sends, 0, source, table)
            if step == 1:
                emit(groups, block, sends, 1, source, table)


def carry_kernel(section, current, passed, carry):
    delay = lax.axis_index("delay")

    @pl.when(delay == section)
    def _():
        carry[...] = current[...]

    @pl.when(delay != section)
    def _():
        carry[...] = passed[...]


def last_kernel(groups, block, step, sheet, column, incident, matrix, aside, *refs):
    blocks, older, refs = refs[:groups], refs[groups : 2 * groups], refs[2 * groups :]
    terms, now = refs[:-1], refs[-1]
    driving = driving_of(incident, step, terms)
    driving = driving - product(matrix, blocks, 0, block) - product(aside, older, 1, block)
    now[...] = law_of(driving, sheet, column)


def choose_kernel(plan, *refs):
    sources, out = refs[:-1], refs[-1]
    rows = sources[0].shape[0]
    chip = lax.axis_index("delay") // 2
    for z, chosen in enumerate(plan):

        @pl.when(chip == z)
        def _():
            for place, index in enumerate(chosen):
                out[place * rows : (place + 1) * rows, :] = sources[index][...]


def out_kernel(early, early_other, late, late_other, out, sems):
    split = early.shape[0]

    def write(first, second):
        copies = (
            pltpu.make_async_copy(first, out.at[:split], sems.at[0]),
            pltpu.make_async_copy(second, out.at[split:], sems.at[1]),
        )
        for copy in copies:
            copy.start()
        for copy in copies:
            copy.wait()

    odd = lax.axis_index("delay") % 2

    @pl.when(odd == 0)
    def _():
        write(early, late)

    @pl.when(odd == 1)
    def _():
        write(early_other, late_other)


def local(retarded, block_row, block_count, send_pick, history, incident, self_block, sheet_diag):
    groups = lax.axis_size("group")
    delays = lax.axis_size("delay")
    chips = delays // 2
    weights = retarded[0]
    depth, block = weights.shape[1], weights.shape[-1]
    rows, columns = history.shape[1:]
    shape = jax.ShapeDtypeStruct
    piece = lambda parts=1: shape((parts * block, columns), BF16)
    many = lambda count: shape((count * rows, columns), BF16)
    whole, wide_whole = many(1), shape((rows, columns), F32)
    bind = functools.partial

    def along(array, pairs):
        return lax.ppermute(array, "delay", pairs)

    def swap(array):
        return along(array, [(d, d ^ 1) for d in range(delays)])

    def shift(array):
        return along(array, [(d, (d + 1) % delays) for d in range(delays)])

    def exchange(sends):
        got = [sends[0]]
        for hop in range(1, groups):
            pairs = [(g, peer_of(g, hop, groups)) for g in range(groups)]
            got.append(lax.ppermute(sends[hop], "group", pairs))
        return got

    def run(kernel, out_shape, scalars, arrays, spare=2):
        return call(kernel, out_shape, scalars, arrays, spare)

    def staged(chip):
        stride, came = 1, None
        while stride < chips:
            if came is not None:
                (chip,) = run(plus_kernel, [whole], (), (chip, came))
            pairs = [(2 * z, 2 * (z - stride)) for z in range(stride, chips, 2 * stride)]
            came = along(chip, pairs)
            stride *= 2
        return [chip, came]

    def direct(chip):
        return [chip] + [along(chip, [(2 * z, 0)]) for z in range(1, chips)]

    h1 = shift(history[0])
    listed = jnp.clip(block_row, 0, rows // block - 1)
    pick = lambda arrays: run(
        bind(pick_kernel, groups, block, len(arrays)), [piece(len(arrays))] * groups, (send_pick,), arrays
    )
    term = lambda firsts, blocks: run(bind(term_kernel, groups, block, firsts), many(len(firsts)), (), (dense, *blocks))

    blocks = exchange(pick((history[0],)))
    dense = run(
        bind(dense_kernel, groups, block, depth),
        shape((rows, groups * block), BF16), (listed, block_count), (weights,),
    )
    h2 = shift(h1)
    mine = term((0,), blocks)
    (chip,) = run(plus_kernel, [whole], (), (mine, swap(mine)))
    field0 = staged(chip)
    blocks = exchange(pick((h1, h2)))
    h3 = shift(h2)
    sheet, column = run(
        sheet_kernel, [shape((rows, rows), BF16), wide_whole], (), (self_block, sheet_diag[None, :]), 20
    )
    mine = term((1, 2), blocks)
    chip1, chip2 = run(plus_kernel, [whole, whole], (), (mine, swap(mine)))
    field1, field2 = direct(chip1), staged(chip2)
    other = swap(send_pick)
    aside = swap(dense)

    law = (sheet, column, incident)
    found, slots = [], []

    def stepped(step, fields, extra, parts):
        current, *sends = run(
            bind(step_kernel, groups, block, step, len(fields)),
            [whole] + [piece(parts)] * groups, (send_pick, other), (*law, *fields, *extra),
        )
        found.append(current)
        return sends

    def pass_on(core=1):
        handed = array = swap(found[-1]) if core else found[-1]
        if slots:
            array = run(bind(carry_kernel, core), whole, (), (array, slots[-1]))
        pairs = [(max(2 * z, core), 2 * z + 2) for z in range(chips - 1)]
        slots.append(along(array, pairs))
        return handed

    def near_of(blocks, first):
        return run(bind(near_kernel, groups, block, first), [wide_whole, whole], (), (dense, *blocks))

    blocks = exchange(stepped(0, field0, (h3,), 1))
    handed = pass_on()
    wide, narrow = near_of(blocks, 3)
    (chip,) = run(plus_kernel, [whole], (), (narrow, swap(narrow)))
    field3 = staged(chip)
    older = exchange(stepped(1, (*field1, wide), (handed, slots[0]), 2))
    pass_on()
    wide, narrow = near_of(older, 1)
    partner = swap(narrow)
    second = along(narrow, [(2, 0)])
    blocks = exchange(stepped(2, (*field2, wide, partner), (), 1))
    pass_on(0)
    found.append(
        run(
            bind(last_kernel, groups, block, 3), whole, (),
            (*law, dense, aside, *blocks, *older, *field3, second),
        )
    )
    carry = run(bind(carry_kernel, 0), whole, (), (found[-1], slots[-1]))
    reach = [STEPS - 1 - step for step in range(STEPS)]
    heads = [z for z in reach if z < chips]
    finals = []
    for k in range(1, chips):
        pairs = [(2 * z, 2 * (z + k)) for z in heads if z + k < chips]
        finals.append(along(found[-1] if len(pairs) == 1 else carry, pairs))

    def origin(step, z):
        beyond = z - reach[step]
        if z == 0:
            return found[step]
        return finals[beyond - 1] if beyond > 0 else slots[step + z - 1]

    def chosen(steps):
        sources, plan = [], []
        for z in range(chips):
            plan.append([])
            for step in steps:
                array = origin(step, z)
                known = [k for k, source in enumerate(sources) if source is array]
                if not known:
                    sources.append(array)
                plan[-1].append(known[0] if known else len(sources) - 1)
        return run(bind(choose_kernel, plan), many(len(steps)), (), sources)

    ready = [s for s in range(STEPS) if chips - 1 <= reach[s]] or [0]
    early = chosen(ready)
    early_other = swap(early)
    late = chosen([s for s in range(STEPS) if s not in ready])
    late_other = swap(late)
    out = pl.pallas_call(
        out_kernel,
        out_shape=many(STEPS),
        in_specs=[VMEM] * 4,
        out_specs=pl.BlockSpec(memory_space=pl.ANY),
        scratch_shapes=[pltpu.SemaphoreType.DMA((2,))],
        compiler_params=pltpu.CompilerParams(vmem_limit_bytes=4 << 20),
    )(early, early_other, late, late_other)
    return out.reshape(STEPS, rows, columns)


def solution(mesh):
    placed = (
        P("delay", "group", None, None, None),
        P("delay", "group", None),
        P("delay", "group"),
        P("delay", None, None),
        P("delay", "group", None),
        P(None, "group", None),
        P("group", None),
        P("group"),
    )

    return jax.shard_map(local, mesh=mesh, in_specs=placed, out_specs=P(None, "group", None), check_vma=False)
```
